512 devices in a mesh: row: 8 (over z_lo, core), bulk: 64 (over z_hi, x, y).
Axes of the slice: x: 4, y: 8, z: 8 (z_hi: 2, z_lo: 4; z = z_hi * 4 + z_lo), core: 2. Of those that a mesh axis runs over, the one named last changes fastest.
Arguments:
- residual_in: float32 [2048, 65536], P('row', 'bulk'), may hold values from -6 to 6
- amplitudes: float32 [2048, 2048], P('row', 'bulk'), may hold values from -6 to 6
- integral_tiles: float32 [4096, 128, 128], P('bulk', 'row'), may hold values from -0.1875 to 0.1875
- tile_reader: int32 [4096, 1], P('bulk'), may hold values from 0 to 63; in each aligned block of 64 rows (0 to 63, 64 to 127, ...) at most 2 rows name the same one
- tile_k: int32 [4096], P('bulk'), may hold values from 0 to 15
- tile_column: int32 [4096], P('bulk'), may hold values from 0 to 7
Outputs:
- residual_out: float32 [2048, 65536], P('row', 'bulk')
The draws below stay inside these ranges and needn't reach their ends.
Inputs may be any that keep to these rules, and one draw needn't show every extreme that they name: `tile_reader`: among the 64 tiles stored on one index of bulk (aligned blocks of 64 entries), at most 2 name the same reader; some block has exactly 2 for some reader.
All inputs are finite; a program needn't handle non-finite values.
Results may differ from the reference program's by a relative error of at most 0.0003.
Values sent between devices are 32-bit elements; how exact they have to be, the bound alone decides.
A program may use at most 64 MiB of HBM per device.

```python
import math
import jax
import jax.numpy as jnp
import numpy as np
from jax import lax

TILE = 128
KT = 16
CT = 8
SLOT = 2
NS = 64
ROWS = 2048
COLS = 512
NTILES = 4096
N_BULK = 64


def set_ends(entries, stream_key, smallest, largest):
    place = [jax.random.randint(jax.random.fold_in(stream_key, axis), (), 0, length) for axis, length in enumerate(entries.shape)]
    main_axis = entries.shape.index(max(entries.shape))
    beside = place[:main_axis] + [(place[main_axis] + 1) % entries.shape[main_axis]] + place[main_axis + 1:]
    return entries.at[tuple(place)].set(smallest).at[tuple(beside)].set(largest)


def block_levels(key, shape, pieces, low, largest):
    gain = 1.0
    for dim, parts in pieces:
        draws = jax.random.uniform(jax.random.fold_in(jax.random.fold_in(key, 6), dim), (parts,), jnp.float32, low / len(pieces), largest / len(pieces))
        gain = gain * jnp.repeat(jnp.exp(draws), shape[dim] // parts).reshape((-1,) + (1,) * (len(shape) - 1 - dim))
    return gain


def routed_block(rng, own, number, rows, number_of, top, bound, lean):
    ranking = jax.random.permutation(rng, number_of)
    heavy_load, ordinary = load_shares(number_of, rows * top, bound, lean, True), load_shares(number_of, rows * top, bound, lean, False)
    places = jnp.arange(number_of)

    def named(lengths, rotation):
        used = int((lengths > 0).sum())
        fixed = max(1, used // 4)
        moved = fixed + (places - fixed + rotation * (used - fixed)) % max(1, number_of - fixed)
        return jnp.zeros((number_of,), jnp.int32).at[ranking[jnp.where(places < fixed, places, moved)]].set(jnp.asarray(lengths, jnp.int32))

    lengths = jnp.where(number % 4 == 0, named(heavy_load, number // 4), named(ordinary, number - number // 4 - 1))
    mixed = jax.random.permutation(jax.random.fold_in(own, 3), number_of)
    giver, receiver = mixed[0:number_of // 2 * 2:2], mixed[1:number_of // 2 * 2:2]
    margin = jnp.minimum(lengths[giver] - 1, bound - lengths[receiver]) // 2
    margin = jnp.where((giver == ranking[0]) | (receiver == ranking[0]) | (lengths[receiver] == 0), 0, jnp.maximum(margin, 0))
    moved = jax.random.randint(jax.random.fold_in(own, 4), (number_of // 2,), 0, 1 << 20) % (margin + 1)
    lengths = lengths.at[giver].add(-moved).at[receiver].add(moved)
    items = jnp.searchsorted(jnp.cumsum(lengths), jnp.arange(rows * top), side="right").astype(jnp.int32)
    grid = items.reshape(top, rows).T
    grid = grid[jax.random.permutation(jax.random.fold_in(own, 1), rows)]
    rotation = jax.random.randint(jax.random.fold_in(own, 2), (rows, 1), 0, top)
    return jnp.take_along_axis(grid, (jnp.arange(top)[None, :] + rotation) % top, axis=1)


def load_shares(count, total, bound, slope, full):
    loads = [(1 << 20) // math.isqrt(rank ** slope) + 1 for rank in range(1, count + 1)]
    largest = bound if full else min(bound, max(-(-total // count), total * loads[0] // sum(loads)))
    least = 1 if total - largest >= count - 1 else 0
    given, surplus = [largest] + [least] * (count - 1), total - largest - least * (count - 1)
    while surplus > 0:
        movable = [i for i in range(1, count) if given[i] < largest] or [i for i in range(1, count) if given[i] < bound]
        pool, remaining = sum([loads[i] for i in movable]), surplus
        for i in movable:
            extra = min(bound - given[i], max(1, remaining * loads[i] // pool), surplus)
            given[i] = given[i] + extra
            surplus = surplus - extra
    return np.array(given)


def scatter_about(rng, extent, width, most, cuts=(), held_as=jnp.bfloat16):
    factor_of = block_levels(rng, extent, cuts, -0.22, 0.18) if cuts else 1.0
    result = jax.random.normal(rng, extent, jnp.float32) * width * factor_of
    return jnp.minimum(jnp.maximum(result, -most), most).astype(held_as)


def setup_inputs(seed: int = 0) -> dict:
    splits = jax.random.split(jax.random.key(seed), 7)
    residual_in = scatter_about(splits[0], (ROWS, COLS * TILE), 1.0, 6.0, ((0, 8), (1, 64)), jnp.float32)
    amplitudes = scatter_about(splits[1], (ROWS, KT * TILE), 1.0, 6.0, ((0, 8), (1, 64)), jnp.float32)
    integral_tiles = scatter_about(splits[2], (NTILES, TILE, TILE), (NS * TILE // CT) ** -0.5, 0.1875, ((0, 64), (1, 8)), jnp.float32)
    tile_reader_keys = jax.random.split(jax.random.fold_in(splits[3], 1), NTILES // NS)
    tile_reader_turns = jax.random.permutation(jax.random.fold_in(splits[3], 3), NTILES // NS)
    tile_reader = jax.vmap(lambda own, number: routed_block(jax.random.fold_in(splits[3], 2), own, number, NS, N_BULK, 1, SLOT, 1))(tile_reader_keys, tile_reader_turns).reshape((NTILES, 1))
    tile_k = set_ends(jax.random.randint(splits[4], (NTILES,), 0, KT), jax.random.fold_in(splits[4], 1), 0, KT - 1).astype(jnp.int32)
    tile_column = set_ends(jax.random.randint(splits[5], (NTILES,), 0, CT), jax.random.fold_in(splits[5], 1), 0, CT - 1).astype(jnp.int32)
    return dict(residual_in=residual_in, amplitudes=amplitudes, integral_tiles=integral_tiles, tile_reader=tile_reader, tile_k=tile_k, tile_column=tile_column)


def reference(residual_in, amplitudes, integral_tiles, tile_reader, tile_k, tile_column):
    readers = tile_reader[:, 0]

    def per_reader(target):
        chosen = readers == target
        blocks = jnp.where(chosen[:, None, None], integral_tiles, jnp.zeros_like(integral_tiles))
        placed = jnp.zeros((KT, CT, TILE, TILE), integral_tiles.dtype).at[tile_k, tile_column].add(blocks)
        dense_block = placed.transpose(0, 2, 1, 3).reshape(KT * TILE, CT * TILE)
        return jnp.dot(amplitudes, dense_block, precision=lax.Precision.HIGHEST)

    columns = lax.map(per_reader, jnp.arange(N_BULK, dtype=jnp.int32))
    columns = columns.transpose(1, 0, 2).reshape(ROWS, N_BULK * CT * TILE)
    return residual_in + columns
```

```python
import jax
import jax.numpy as jnp
import numpy as np
from jax import lax
from jax.sharding import Mesh, PartitionSpec as P

KT = 16
CT = 8
SLOT = 2


def bucket_slots(tile_reader, tile_k, tile_column, targets, slots):
    readers = tile_reader[:, 0]
    matches = (readers[:, None] == jnp.arange(targets, dtype=jnp.int32)[None, :]).astype(jnp.int32)
    ordinal = jnp.cumsum(matches, axis=0) - matches
    position = jnp.sum(ordinal * matches, axis=1)
    select = matches.T[:, None, :] * (
        position[None, None, :] == jnp.arange(slots, dtype=jnp.int32)[None, :, None]
    ).astype(jnp.int32)
    filled = jnp.sum(select, axis=2)
    local_index = jnp.sum(select * jnp.arange(readers.shape[0], dtype=jnp.int32)[None, None, :], axis=2)
    slot_tile = jnp.sum(select * tile_k[None, None, :], axis=2) + filled - 1
    slot_column = jnp.sum(select * tile_column[None, None, :], axis=2) + filled - 1
    return filled, local_index, slot_tile, slot_column


def local(residual_in, amplitudes, integral_tiles, tile_reader, tile_k, tile_column):
    targets = lax.axis_size("bulk")
    height, width = integral_tiles.shape[1], integral_tiles.shape[2]
    filled, local_index, slot_tile, slot_column = bucket_slots(
        tile_reader, tile_k, tile_column, targets, SLOT
    )
    picked = jnp.take(integral_tiles, local_index.reshape(-1), axis=0)
    picked = jnp.where(filled.reshape(-1)[:, None, None] > 0, picked, 0.0)
    outgoing = picked.reshape(targets, SLOT, height, width)
    arrived, arrived_tile, arrived_column = (
        lax.all_to_all(outgoing, "bulk", split_axis=0, concat_axis=0, tiled=True),
        lax.all_to_all(slot_tile, "bulk", split_axis=0, concat_axis=0, tiled=True),
        lax.all_to_all(slot_column, "bulk", split_axis=0, concat_axis=0, tiled=True),
    )
    arrived = arrived.reshape(targets * SLOT, height * width)
    position = arrived_tile.reshape(-1) * CT + arrived_column.reshape(-1)
    table = (position[None, :] == jnp.arange(KT * CT, dtype=jnp.int32)[:, None]).astype(jnp.float32)
    placed = jnp.dot(table, arrived, precision=lax.Precision.HIGHEST)
    placed = placed.reshape(KT, CT, height, width).transpose(0, 2, 1, 3).reshape(KT * height, CT * width)
    gathered = lax.all_gather(placed, "zl", axis=0, tiled=False)
    gathered = lax.all_gather(gathered, "core", axis=1, tiled=False)
    dense = gathered.reshape(-1, CT * width)
    amps = lax.all_gather(amplitudes, "bulk", axis=1, tiled=True)
    rows = amps.shape[0]
    groups = gathered.shape[0] * gathered.shape[1]
    amps = amps.reshape(rows, KT, groups, height).transpose(0, 2, 1, 3).reshape(rows, -1)
    return residual_in + jnp.dot(amps, dense, precision=lax.Precision.HIGHEST)


def solution(mesh):
    row_size = mesh.shape["row"]
    devices = np.asarray(mesh.devices).reshape(row_size // 2, 2, mesh.shape["bulk"])
    inner = Mesh(devices, ("zl", "core", "bulk"))
    row = ("zl", "core")
    placed = (
        P(row, "bulk"),
        P(row, "bulk"),
        P("bulk", row, None),
        P("bulk", None),
        P("bulk"),
        P("bulk"),
    )
    return jax.shard_map(
        local, mesh=inner, in_specs=placed, out_specs=P(row, "bulk"), check_vma=False
    )
```

```python
import functools

import jax
import jax.numpy as jnp
import numpy as np
from jax import lax
from jax.experimental import pallas as pl
from jax.experimental.pallas import tpu as pltpu
from jax.sharding import Mesh, PartitionSpec as P

MESH = pl.DeviceIdType.MESH

KT = 16
CT = 8
SLOT = 2


def bucket_slots(tile_reader, tile_k, tile_column, targets, slots):
    readers = tile_reader[:, 0]
    matches = (readers[:, None] == jnp.arange(targets, dtype=jnp.int32)[None, :]).astype(jnp.int32)
    ordinal = jnp.cumsum(matches, axis=0) - matches
    position = jnp.sum(ordinal * matches, axis=1)
    select = matches.T[:, None, :] * (
        position[None, None, :] == jnp.arange(slots, dtype=jnp.int32)[None, :, None]
    ).astype(jnp.int32)
    filled = jnp.sum(select, axis=2)
    local_index = jnp.sum(select * jnp.arange(readers.shape[0], dtype=jnp.int32)[None, None, :], axis=2)
    slot_position = jnp.sum(select * (tile_k * CT + tile_column)[None, None, :], axis=2) + filled - 1
    return filled, local_index, slot_position


def gather_kernel(nz, src_ref, out_ref, local_sem, send_sem, recv_sem):
    zl = lax.axis_index("zl")
    c = lax.axis_index("core")
    b = lax.axis_index("bulk")
    partner = (zl, 1 - c, b)
    left = (zl - 1, c, b)
    right = (zl + 1, c, b)
    has_left = zl > 0
    has_right = zl < nz - 1
    own = zl * 2 + c

    barrier = pltpu.get_barrier_semaphore()
    pl.semaphore_signal(barrier, 1, device_id=partner, device_id_type=MESH)

    @pl.when(has_left)
    def _():
        pl.semaphore_signal(barrier, 1, device_id=left, device_id_type=MESH)

    @pl.when(has_right)
    def _():
        pl.semaphore_signal(barrier, 1, device_id=right, device_id_type=MESH)

    peers = 1 + has_left.astype(jnp.int32) + has_right.astype(jnp.int32)
    pl.semaphore_wait(barrier, peers)

    def copy(src, slot, kind, dev):
        return pltpu.make_async_remote_copy(
            src_ref=src,
            dst_ref=out_ref.at[slot],
            send_sem=send_sem.at[slot, kind],
            recv_sem=recv_sem.at[slot],
            device_id=dev,
            device_id_type=MESH,
        )

    mine = pltpu.make_async_copy(src_ref, out_ref.at[own], local_sem)
    mine.start()
    copy(src_ref, own, 0, partner).start()

    @pl.when(has_left)
    def _():
        copy(src_ref, own, 1, left).start()

    @pl.when(has_right)
    def _():
        copy(src_ref, own, 2, right).start()

    for d in range(1, nz):
        @pl.when(zl - d >= 0)
        def _():
            s = (zl - d) * 2 + c
            copy(out_ref.at[s], s, 0, partner).wait_recv()
            copy(out_ref.at[s], s, 0, partner).start()

            @pl.when(has_right)
            def _():
                copy(out_ref.at[s], s, 2, right).start()

        @pl.when(zl + d <= nz - 1)
        def _():
            s = (zl + d) * 2 + c
            copy(out_ref.at[s], s, 0, partner).wait_recv()
            copy(out_ref.at[s], s, 0, partner).start()

            @pl.when(has_left)
            def _():
                copy(out_ref.at[s], s, 1, left).start()

    for z in range(nz):
        s = z * 2 + (1 - c)
        copy(out_ref.at[s], s, 0, partner).wait_recv()

    mine.wait()
    for z in range(nz):
        s = z * 2 + c
        copy(out_ref.at[s], s, 0, partner).wait_send()

        @pl.when(has_left & (z >= zl))
        def _():
            copy(out_ref.at[s], s, 1, left).wait_send()

        @pl.when(has_right & (z <= zl))
        def _():
            copy(out_ref.at[s], s, 2, right).wait_send()


def row_gather(placed, nz):
    groups = 2 * nz
    return pl.pallas_call(
        functools.partial(gather_kernel, nz),
        out_shape=jax.ShapeDtypeStruct((groups,) + placed.shape, placed.dtype),
        in_specs=[pl.BlockSpec(memory_space=pltpu.VMEM)],
        out_specs=pl.BlockSpec(memory_space=pl.ANY),
        scratch_shapes=[
            pltpu.SemaphoreType.DMA(()),
            pltpu.SemaphoreType.DMA((groups, 3)),
            pltpu.SemaphoreType.DMA((groups,)),
        ],
        compiler_params=pltpu.CompilerParams(collective_id=0, has_side_effects=True),
    )(placed)


def local(residual_in, amplitudes, integral_tiles, tile_reader, tile_k, tile_column):
    targets = lax.axis_size("bulk")
    height, width = integral_tiles.shape[1], integral_tiles.shape[2]
    filled, local_index, slot_position = bucket_slots(
        tile_reader, tile_k, tile_column, targets, SLOT
    )
    picked = jnp.take(integral_tiles, local_index.reshape(-1), axis=0)
    picked = jnp.where(filled.reshape(-1)[:, None, None] > 0, picked, 0.0)
    outgoing = picked.reshape(targets, SLOT, height, width)
    arrived = lax.all_to_all(outgoing, "bulk", split_axis=0, concat_axis=0, tiled=True)
    position = lax.all_to_all(slot_position, "bulk", split_axis=0, concat_axis=0, tiled=True)
    arrived = arrived.reshape(targets * SLOT, height * width)
    position = position.reshape(-1)
    table = (position[None, :] == jnp.arange(KT * CT, dtype=jnp.int32)[:, None]).astype(jnp.float32)
    placed = jnp.dot(table, arrived, precision=lax.Precision.HIGHEST)
    placed = placed.reshape(KT, CT, height, width).transpose(0, 2, 1, 3).reshape(KT * height, CT * width)
    nz = lax.axis_size("zl")
    gathered = row_gather(placed, nz)
    dense = gathered.reshape(-1, CT * width)
    amps = lax.all_gather(amplitudes, "bulk", axis=1, tiled=True)
    rows = amps.shape[0]
    groups = gathered.shape[0]
    amps = amps.reshape(rows, KT, groups, height).transpose(0, 2, 1, 3).reshape(rows, -1)
    return residual_in + jnp.dot(amps, dense, precision=lax.Precision.HIGHEST)


def solution(mesh):
    row_size = mesh.shape["row"]
    devices = np.asarray(mesh.devices).reshape(row_size // 2, 2, mesh.shape["bulk"])
    inner = Mesh(devices, ("zl", "core", "bulk"))
    row = ("zl", "core")
    placed = (
        P(row, "bulk"),
        P(row, "bulk"),
        P("bulk", row, None),
        P("bulk", None),
        P("bulk"),
        P("bulk"),
    )
    return jax.shard_map(
        local, mesh=inner, in_specs=placed, out_specs=P(row, "bulk"), check_vma=False
    )
```

```python
import functools

import jax
import jax.numpy as jnp
import numpy as np
from jax import lax
from jax.experimental import pallas as pl
from jax.experimental.pallas import tpu as pltpu
from jax.sharding import Mesh, PartitionSpec as P

MESH = pl.DeviceIdType.MESH

KT = 16
CT = 8
SLOT = 2


def bucket_slots(tile_reader, tile_k, tile_column, targets, slots):
    readers = tile_reader[:, 0]
    matches = (readers[:, None] == jnp.arange(targets, dtype=jnp.int32)[None, :]).astype(jnp.int32)
    ordinal = jnp.cumsum(matches, axis=0) - matches
    position = jnp.sum(ordinal * matches, axis=1)
    select = matches.T[:, None, :] * (
        position[None, None, :] == jnp.arange(slots, dtype=jnp.int32)[None, :, None]
    ).astype(jnp.int32)
    filled = jnp.sum(select, axis=2)
    local_index = jnp.sum(select * jnp.arange(readers.shape[0], dtype=jnp.int32)[None, None, :], axis=2)
    slot_position = jnp.sum(select * (tile_k * CT + tile_column)[None, None, :], axis=2) + filled - 1
    return filled, local_index, slot_position


def gather_kernel(nz, src_ref, out_ref, local_sem, send_sem, recv_sem):
    zl = lax.axis_index("zl")
    c = lax.axis_index("core")
    b = lax.axis_index("bulk")
    partner = (zl, 1 - c, b)
    left = (zl - 1, c, b)
    right = (zl + 1, c, b)
    has_left = zl > 0
    has_right = zl < nz - 1
    own = zl * 2 + c

    barrier = pltpu.get_barrier_semaphore()
    pl.semaphore_signal(barrier, 1, device_id=partner, device_id_type=MESH)

    @pl.when(has_left)
    def _():
        pl.semaphore_signal(barrier, 1, device_id=left, device_id_type=MESH)

    @pl.when(has_right)
    def _():
        pl.semaphore_signal(barrier, 1, device_id=right, device_id_type=MESH)

    peers = 1 + has_left.astype(jnp.int32) + has_right.astype(jnp.int32)
    pl.semaphore_wait(barrier, peers)

    def copy(src, slot, kind, dev):
        return pltpu.make_async_remote_copy(
            src_ref=src,
            dst_ref=out_ref.at[slot],
            send_sem=send_sem.at[slot, kind],
            recv_sem=recv_sem.at[slot],
            device_id=dev,
            device_id_type=MESH,
        )

    mine = pltpu.make_async_copy(src_ref, out_ref.at[own], local_sem)
    mine.start()
    copy(src_ref, own, 0, partner).start()

    @pl.when(has_left)
    def _():
        copy(src_ref, own, 1, left).start()

    @pl.when(has_right)
    def _():
        copy(src_ref, own, 2, right).start()

    for d in range(1, nz):
        @pl.when(zl - d >= 0)
        def _():
            s = (zl - d) * 2 + c
            copy(out_ref.at[s], s, 0, partner).wait_recv()
            copy(out_ref.at[s], s, 0, partner).start()

            @pl.when(has_right)
            def _():
                copy(out_ref.at[s], s, 2, right).start()

        @pl.when(zl + d <= nz - 1)
        def _():
            s = (zl + d) * 2 + c
            copy(out_ref.at[s], s, 0, partner).wait_recv()
            copy(out_ref.at[s], s, 0, partner).start()

            @pl.when(has_left)
            def _():
                copy(out_ref.at[s], s, 1, left).start()

    for z in range(nz):
        s = z * 2 + (1 - c)
        copy(out_ref.at[s], s, 0, partner).wait_recv()

    mine.wait()
    for z in range(nz):
        s = z * 2 + c
        copy(out_ref.at[s], s, 0, partner).wait_send()

        @pl.when(has_left & (z >= zl))
        def _():
            copy(out_ref.at[s], s, 1, left).wait_send()

        @pl.when(has_right & (z <= zl))
        def _():
            copy(out_ref.at[s], s, 2, right).wait_send()


def row_gather(placed, nz):
    groups = 2 * nz
    return pl.pallas_call(
        functools.partial(gather_kernel, nz),
        out_shape=jax.ShapeDtypeStruct((groups,) + placed.shape, placed.dtype),
        in_specs=[pl.BlockSpec(memory_space=pltpu.VMEM)],
        out_specs=pl.BlockSpec(memory_space=pl.ANY),
        scratch_shapes=[
            pltpu.SemaphoreType.DMA(()),
            pltpu.SemaphoreType.DMA((groups, 3)),
            pltpu.SemaphoreType.DMA((groups,)),
        ],
        compiler_params=pltpu.CompilerParams(collective_id=0, has_side_effects=True),
    )(placed)


def local(residual_in, amplitudes, integral_tiles, tile_reader, tile_k, tile_column):
    targets = lax.axis_size("bulk")
    height, width = integral_tiles.shape[1], integral_tiles.shape[2]
    filled, local_index, slot_position = bucket_slots(
        tile_reader, tile_k, tile_column, targets, SLOT
    )
    picked = jnp.take(integral_tiles, local_index.reshape(-1), axis=0)
    picked = jnp.where(filled.reshape(-1)[:, None, None] > 0, picked, 0.0)
    label = jnp.zeros((targets, 1, width), jnp.float32).at[:, 0, :SLOT].set(
        slot_position.reshape(targets, SLOT).astype(jnp.float32)
    )
    outgoing = jnp.concatenate([picked.reshape(targets, SLOT * height, width), label], axis=1)
    arrived = lax.all_to_all(outgoing, "bulk", split_axis=0, concat_axis=0, tiled=True)
    position = arrived[:, SLOT * height, :SLOT].reshape(-1).astype(jnp.int32)
    arrived = arrived[:, : SLOT * height, :].reshape(targets * SLOT, height * width)
    table = (position[None, :] == jnp.arange(KT * CT, dtype=jnp.int32)[:, None]).astype(jnp.float32)
    placed = jnp.dot(table, arrived, precision=lax.Precision.HIGHEST)
    placed = placed.reshape(KT, CT, height, width).transpose(0, 2, 1, 3).reshape(KT * height, CT * width)
    nz = lax.axis_size("zl")
    gathered = row_gather(placed, nz)
    dense = gathered.reshape(-1, CT * width)
    amps = lax.all_gather(amplitudes, "bulk", axis=1, tiled=True)
    rows = amps.shape[0]
    groups = gathered.shape[0]
    amps = amps.reshape(rows, KT, groups, height).transpose(0, 2, 1, 3).reshape(rows, -1)
    return residual_in + jnp.dot(amps, dense, precision=lax.Precision.HIGHEST)


def solution(mesh):
    row_size = mesh.shape["row"]
    devices = np.asarray(mesh.devices).reshape(row_size // 2, 2, mesh.shape["bulk"])
    inner = Mesh(devices, ("zl", "core", "bulk"))
    row = ("zl", "core")
    placed = (
        P(row, "bulk"),
        P(row, "bulk"),
        P("bulk", row, None),
        P("bulk", None),
        P("bulk"),
        P("bulk"),
    )
    return jax.shard_map(
        local, mesh=inner, in_specs=placed, out_specs=P(row, "bulk"), check_vma=False
    )
```

```python
import functools

import jax
import jax.numpy as jnp
import numpy as np
from jax import lax
from jax.experimental import pallas as pl
from jax.experimental.pallas import tpu as pltpu
from jax.sharding import Mesh, PartitionSpec as P

MESH = pl.DeviceIdType.MESH

KT = 16
CT = 8
SLOT = 2


def bucket_slots(tile_reader, tile_k, tile_column, targets, slots):
    readers = tile_reader[:, 0]
    matches = (readers[:, None] == jnp.arange(targets, dtype=jnp.int32)[None, :]).astype(jnp.int32)
    ordinal = jnp.cumsum(matches, axis=0) - matches
    position = jnp.sum(ordinal * matches, axis=1)
    select = matches.T[:, None, :] * (
        position[None, None, :] == jnp.arange(slots, dtype=jnp.int32)[None, :, None]
    ).astype(jnp.int32)
    filled = jnp.sum(select, axis=2)
    local_index = jnp.sum(select * jnp.arange(readers.shape[0], dtype=jnp.int32)[None, None, :], axis=2)
    slot_position = jnp.sum(select * (tile_k * CT + tile_column)[None, None, :], axis=2) + filled - 1
    return filled, local_index, slot_position


def gather_kernel(nz, src_ref, out_ref, local_sem, send_sem, recv_sem):
    zl = lax.axis_index("zl")
    c = lax.axis_index("core")
    b = lax.axis_index("bulk")
    partner = (zl, 1 - c, b)
    left = (zl - 1, c, b)
    right = (zl + 1, c, b)
    has_left = zl > 0
    has_right = zl < nz - 1
    own = zl * 2 + c

    barrier = pltpu.get_barrier_semaphore()
    pl.semaphore_signal(barrier, 1, device_id=partner, device_id_type=MESH)

    @pl.when(has_left)
    def _():
        pl.semaphore_signal(barrier, 1, device_id=left, device_id_type=MESH)

    @pl.when(has_right)
    def _():
        pl.semaphore_signal(barrier, 1, device_id=right, device_id_type=MESH)

    peers = 1 + has_left.astype(jnp.int32) + has_right.astype(jnp.int32)
    pl.semaphore_wait(barrier, peers)

    def copy(src, slot, kind, dev):
        return pltpu.make_async_remote_copy(
            src_ref=src,
            dst_ref=out_ref.at[slot],
            send_sem=send_sem.at[slot, kind],
            recv_sem=recv_sem.at[slot],
            device_id=dev,
            device_id_type=MESH,
        )

    mine = pltpu.make_async_copy(src_ref, out_ref.at[own], local_sem)
    mine.start()
    copy(src_ref, own, 0, partner).start()

    @pl.when(has_left)
    def _():
        copy(src_ref, own, 1, left).start()

    @pl.when(has_right)
    def _():
        copy(src_ref, own, 2, right).start()

    for d in range(1, nz):
        @pl.when(zl - d >= 0)
        def _():
            s = (zl - d) * 2 + c
            copy(out_ref.at[s], s, 0, partner).wait_recv()
            copy(out_ref.at[s], s, 0, partner).start()

            @pl.when(has_right)
            def _():
                copy(out_ref.at[s], s, 2, right).start()

        @pl.when(zl + d <= nz - 1)
        def _():
            s = (zl + d) * 2 + c
            copy(out_ref.at[s], s, 0, partner).wait_recv()
            copy(out_ref.at[s], s, 0, partner).start()

            @pl.when(has_left)
            def _():
                copy(out_ref.at[s], s, 1, left).start()

    for z in range(nz):
        s = z * 2 + (1 - c)
        copy(out_ref.at[s], s, 0, partner).wait_recv()

    mine.wait()
    for z in range(nz):
        s = z * 2 + c
        copy(out_ref.at[s], s, 0, partner).wait_send()

        @pl.when(has_left & (z >= zl))
        def _():
            copy(out_ref.at[s], s, 1, left).wait_send()

        @pl.when(has_right & (z <= zl))
        def _():
            copy(out_ref.at[s], s, 2, right).wait_send()


def row_gather(placed, nz):
    groups = 2 * nz
    return pl.pallas_call(
        functools.partial(gather_kernel, nz),
        out_shape=jax.ShapeDtypeStruct((groups,) + placed.shape, placed.dtype),
        in_specs=[pl.BlockSpec(memory_space=pltpu.VMEM)],
        out_specs=pl.BlockSpec(memory_space=pl.ANY),
        scratch_shapes=[
            pltpu.SemaphoreType.DMA(()),
            pltpu.SemaphoreType.DMA((groups, 3)),
            pltpu.SemaphoreType.DMA((groups,)),
        ],
        compiler_params=pltpu.CompilerParams(collective_id=0, has_side_effects=True),
    )(placed)


def exchange_kernel(nb, src_ref, out_ref, local_sem, send_sem, recv_sem):
    zl = lax.axis_index("zl")
    c = lax.axis_index("core")
    me = lax.axis_index("bulk")

    barrier = pltpu.get_barrier_semaphore()

    def greet(p, carry):
        pl.semaphore_signal(barrier, 1, device_id=(zl, c, lax.rem(me + p, nb)), device_id_type=MESH)
        return carry

    lax.fori_loop(1, nb, greet, 0)
    pl.semaphore_wait(barrier, nb - 1)

    mine = pltpu.make_async_copy(src_ref.at[me], out_ref.at[me], local_sem)
    mine.start()

    def copy(p, dest):
        return pltpu.make_async_remote_copy(
            src_ref=src_ref.at[dest],
            dst_ref=out_ref.at[me],
            send_sem=send_sem.at[p],
            recv_sem=recv_sem.at[me],
            device_id=(zl, c, dest),
            device_id_type=MESH,
        )

    def send(p, carry):
        copy(p, lax.rem(me + p, nb)).start()
        return carry

    lax.fori_loop(1, nb, send, 0)

    def receive(p, carry):
        source = lax.rem(me + nb - p, nb)
        pltpu.make_async_remote_copy(
            src_ref=src_ref.at[source],
            dst_ref=out_ref.at[source],
            send_sem=send_sem.at[p],
            recv_sem=recv_sem.at[source],
            device_id=(zl, c, source),
            device_id_type=MESH,
        ).wait_recv()
        return carry

    lax.fori_loop(1, nb, receive, 0)
    mine.wait()

    def sent(p, carry):
        copy(p, lax.rem(me + p, nb)).wait_send()
        return carry

    lax.fori_loop(1, nb, sent, 0)


def bulk_exchange(outgoing, nb):
    return pl.pallas_call(
        functools.partial(exchange_kernel, nb),
        out_shape=jax.ShapeDtypeStruct(outgoing.shape, outgoing.dtype),
        in_specs=[pl.BlockSpec(memory_space=pltpu.VMEM)],
        out_specs=pl.BlockSpec(memory_space=pltpu.VMEM),
        scratch_shapes=[
            pltpu.SemaphoreType.DMA(()),
            pltpu.SemaphoreType.DMA((nb,)),
            pltpu.SemaphoreType.DMA((nb,)),
        ],
        compiler_params=pltpu.CompilerParams(collective_id=1, has_side_effects=True),
    )(outgoing)


def local(residual_in, amplitudes, integral_tiles, tile_reader, tile_k, tile_column):
    targets = lax.axis_size("bulk")
    height, width = integral_tiles.shape[1], integral_tiles.shape[2]
    filled, local_index, slot_position = bucket_slots(
        tile_reader, tile_k, tile_column, targets, SLOT
    )
    picked = jnp.take(integral_tiles, local_index.reshape(-1), axis=0)
    picked = jnp.where(filled.reshape(-1)[:, None, None] > 0, picked, 0.0)
    label = jnp.zeros((targets, 1, width), jnp.float32).at[:, 0, :SLOT].set(
        slot_position.reshape(targets, SLOT).astype(jnp.float32)
    )
    outgoing = jnp.concatenate([picked.reshape(targets, SLOT * height, width), label], axis=1)
    arrived = bulk_exchange(outgoing, targets)
    position = arrived[:, SLOT * height, :SLOT].reshape(-1).astype(jnp.int32)
    arrived = arrived[:, : SLOT * height, :].reshape(targets * SLOT, height * width)
    table = (position[None, :] == jnp.arange(KT * CT, dtype=jnp.int32)[:, None]).astype(jnp.float32)
    placed = jnp.dot(table, arrived, precision=lax.Precision.HIGHEST)
    placed = placed.reshape(KT, CT, height, width).transpose(0, 2, 1, 3).reshape(KT * height, CT * width)
    nz = lax.axis_size("zl")
    gathered = row_gather(placed, nz)
    dense = gathered.reshape(-1, CT * width)
    amps = lax.all_gather(amplitudes, "bulk", axis=1, tiled=True)
    rows = amps.shape[0]
    groups = gathered.shape[0]
    amps = amps.reshape(rows, KT, groups, height).transpose(0, 2, 1, 3).reshape(rows, -1)
    return residual_in + jnp.dot(amps, dense, precision=lax.Precision.HIGHEST)


def solution(mesh):
    row_size = mesh.shape["row"]
    devices = np.asarray(mesh.devices).reshape(row_size // 2, 2, mesh.shape["bulk"])
    inner = Mesh(devices, ("zl", "core", "bulk"))
    row = ("zl", "core")
    placed = (
        P(row, "bulk"),
        P(row, "bulk"),
        P("bulk", row, None),
        P("bulk", None),
        P("bulk"),
        P("bulk"),
    )
    return jax.shard_map(
        local, mesh=inner, in_specs=placed, out_specs=P(row, "bulk"), check_vma=False
    )
```

```python
import functools

import jax
import jax.numpy as jnp
import numpy as np
from jax import lax
from jax.experimental import pallas as pl
from jax.experimental.pallas import tpu as pltpu
from jax.sharding import Mesh, PartitionSpec as P

MESH = pl.DeviceIdType.MESH

KT = 16
CT = 8
SLOT = 2


def bucket_slots(tile_reader, tile_k, tile_column, targets, slots):
    readers = tile_reader[:, 0]
    matches = (readers[:, None] == jnp.arange(targets, dtype=jnp.int32)[None, :]).astype(jnp.int32)
    ordinal = jnp.cumsum(matches, axis=0) - matches
    position = jnp.sum(ordinal * matches, axis=1)
    select = matches.T[:, None, :] * (
        position[None, None, :] == jnp.arange(slots, dtype=jnp.int32)[None, :, None]
    ).astype(jnp.int32)
    filled = jnp.sum(select, axis=2)
    local_index = jnp.sum(select * jnp.arange(readers.shape[0], dtype=jnp.int32)[None, None, :], axis=2)
    slot_position = jnp.sum(select * (tile_k * CT + tile_column)[None, None, :], axis=2) + filled - 1
    return filled, local_index, slot_position


def gather_kernel(nz, src_ref, out_ref, local_sem, send_sem, recv_sem):
    zl = lax.axis_index("zl")
    c = lax.axis_index("core")
    b = lax.axis_index("bulk")
    partner = (zl, 1 - c, b)
    left = (zl - 1, c, b)
    right = (zl + 1, c, b)
    has_left = zl > 0
    has_right = zl < nz - 1
    own = zl * 2 + c

    barrier = pltpu.get_barrier_semaphore()
    pl.semaphore_signal(barrier, 1, device_id=partner, device_id_type=MESH)

    @pl.when(has_left)
    def _():
        pl.semaphore_signal(barrier, 1, device_id=left, device_id_type=MESH)

    @pl.when(has_right)
    def _():
        pl.semaphore_signal(barrier, 1, device_id=right, device_id_type=MESH)

    peers = 1 + has_left.astype(jnp.int32) + has_right.astype(jnp.int32)
    pl.semaphore_wait(barrier, peers)

    def copy(src, slot, kind, dev):
        return pltpu.make_async_remote_copy(
            src_ref=src,
            dst_ref=out_ref.at[slot],
            send_sem=send_sem.at[slot, kind],
            recv_sem=recv_sem.at[slot],
            device_id=dev,
            device_id_type=MESH,
        )

    mine = pltpu.make_async_copy(src_ref, out_ref.at[own], local_sem)
    mine.start()
    copy(src_ref, own, 0, partner).start()

    @pl.when(has_left)
    def _():
        copy(src_ref, own, 1, left).start()

    @pl.when(has_right)
    def _():
        copy(src_ref, own, 2, right).start()

    for d in range(1, nz):
        @pl.when(zl - d >= 0)
        def _():
            s = (zl - d) * 2 + c
            copy(out_ref.at[s], s, 0, partner).wait_recv()
            copy(out_ref.at[s], s, 0, partner).start()

            @pl.when(has_right)
            def _():
                copy(out_ref.at[s], s, 2, right).start()

        @pl.when(zl + d <= nz - 1)
        def _():
            s = (zl + d) * 2 + c
            copy(out_ref.at[s], s, 0, partner).wait_recv()
            copy(out_ref.at[s], s, 0, partner).start()

            @pl.when(has_left)
            def _():
                copy(out_ref.at[s], s, 1, left).start()

    for z in range(nz):
        s = z * 2 + (1 - c)
        copy(out_ref.at[s], s, 0, partner).wait_recv()

    mine.wait()
    for z in range(nz):
        s = z * 2 + c
        copy(out_ref.at[s], s, 0, partner).wait_send()

        @pl.when(has_left & (z >= zl))
        def _():
            copy(out_ref.at[s], s, 1, left).wait_send()

        @pl.when(has_right & (z <= zl))
        def _():
            copy(out_ref.at[s], s, 2, right).wait_send()


def row_gather(placed, nz):
    groups = 2 * nz
    return pl.pallas_call(
        functools.partial(gather_kernel, nz),
        out_shape=jax.ShapeDtypeStruct((groups,) + placed.shape, placed.dtype),
        in_specs=[pl.BlockSpec(memory_space=pltpu.VMEM)],
        out_specs=pl.BlockSpec(memory_space=pltpu.VMEM),
        scratch_shapes=[
            pltpu.SemaphoreType.DMA(()),
            pltpu.SemaphoreType.DMA((groups, 3)),
            pltpu.SemaphoreType.DMA((groups,)),
        ],
        compiler_params=pltpu.CompilerParams(collective_id=0, has_side_effects=True),
    )(placed)


def exchange_kernel(nb, src_ref, out_ref, local_sem, send_sem, recv_sem):
    zl = lax.axis_index("zl")
    c = lax.axis_index("core")
    me = lax.axis_index("bulk")

    barrier = pltpu.get_barrier_semaphore()

    def greet(p, carry):
        pl.semaphore_signal(barrier, 1, device_id=(zl, c, lax.rem(me + p, nb)), device_id_type=MESH)
        return carry

    lax.fori_loop(1, nb, greet, 0)
    pl.semaphore_wait(barrier, nb - 1)

    mine = pltpu.make_async_copy(src_ref.at[me], out_ref.at[me], local_sem)
    mine.start()

    def copy(p, dest):
        return pltpu.make_async_remote_copy(
            src_ref=src_ref.at[dest],
            dst_ref=out_ref.at[me],
            send_sem=send_sem.at[p],
            recv_sem=recv_sem.at[me],
            device_id=(zl, c, dest),
            device_id_type=MESH,
        )

    def send(p, carry):
        copy(p, lax.rem(me + p, nb)).start()
        return carry

    lax.fori_loop(1, nb, send, 0)

    def receive(p, carry):
        source = lax.rem(me + nb - p, nb)
        pltpu.make_async_remote_copy(
            src_ref=src_ref.at[source],
            dst_ref=out_ref.at[source],
            send_sem=send_sem.at[p],
            recv_sem=recv_sem.at[source],
            device_id=(zl, c, source),
            device_id_type=MESH,
        ).wait_recv()
        return carry

    lax.fori_loop(1, nb, receive, 0)
    mine.wait()

    def sent(p, carry):
        copy(p, lax.rem(me + p, nb)).wait_send()
        return carry

    lax.fori_loop(1, nb, sent, 0)


def bulk_exchange(outgoing, nb):
    return pl.pallas_call(
        functools.partial(exchange_kernel, nb),
        out_shape=jax.ShapeDtypeStruct(outgoing.shape, outgoing.dtype),
        in_specs=[pl.BlockSpec(memory_space=pltpu.VMEM)],
        out_specs=pl.BlockSpec(memory_space=pltpu.VMEM),
        scratch_shapes=[
            pltpu.SemaphoreType.DMA(()),
            pltpu.SemaphoreType.DMA((nb,)),
            pltpu.SemaphoreType.DMA((nb,)),
        ],
        compiler_params=pltpu.CompilerParams(collective_id=1, has_side_effects=True),
    )(outgoing)


def local(residual_in, amplitudes, integral_tiles, tile_reader, tile_k, tile_column):
    targets = lax.axis_size("bulk")
    height, width = integral_tiles.shape[1], integral_tiles.shape[2]
    filled, local_index, slot_position = bucket_slots(
        tile_reader, tile_k, tile_column, targets, SLOT
    )
    picked = jnp.take(integral_tiles, local_index.reshape(-1), axis=0)
    picked = jnp.where(filled.reshape(-1)[:, None, None] > 0, picked, 0.0)
    label = jnp.zeros((targets, 1, width), jnp.float32).at[:, 0, :SLOT].set(
        slot_position.reshape(targets, SLOT).astype(jnp.float32)
    )
    outgoing = jnp.concatenate([picked.reshape(targets, SLOT * height, width), label], axis=1)
    arrived = bulk_exchange(outgoing, targets)
    position = arrived[:, SLOT * height, :SLOT].reshape(-1).astype(jnp.int32)
    arrived = arrived[:, : SLOT * height, :].reshape(targets * SLOT, height * width)
    table = (position[None, :] == jnp.arange(KT * CT, dtype=jnp.int32)[:, None]).astype(jnp.float32)
    placed = jnp.dot(table, arrived, precision=lax.Precision.HIGHEST)
    placed = placed.reshape(KT, CT, height, width).transpose(0, 2, 1, 3).reshape(KT * height, CT * width)
    nz = lax.axis_size("zl")
    gathered = row_gather(placed, nz)
    dense = gathered.reshape(-1, CT * width)
    amps = lax.all_gather(amplitudes, "bulk", axis=1, tiled=True)
    rows = amps.shape[0]
    groups = gathered.shape[0]
    amps = amps.reshape(rows, KT, groups, height).transpose(0, 2, 1, 3).reshape(rows, -1)
    return residual_in + jnp.dot(amps, dense, precision=lax.Precision.HIGH)


def solution(mesh):
    row_size = mesh.shape["row"]
    devices = np.asarray(mesh.devices).reshape(row_size // 2, 2, mesh.shape["bulk"])
    inner = Mesh(devices, ("zl", "core", "bulk"))
    row = ("zl", "core")
    placed = (
        P(row, "bulk"),
        P(row, "bulk"),
        P("bulk", row, None),
        P("bulk", None),
        P("bulk"),
        P("bulk"),
    )
    return jax.shard_map(
        local, mesh=inner, in_specs=placed, out_specs=P(row, "bulk"), check_vma=False
    )
```

```python
import functools

import jax
import jax.numpy as jnp
import numpy as np
from jax import lax
from jax.experimental import pallas as pl
from jax.experimental.pallas import tpu as pltpu
from jax.sharding import Mesh, PartitionSpec as P

MESH = pl.DeviceIdType.MESH

KT = 16
CT = 8
SLOT = 2


def bucket_slots(tile_reader, tile_k, tile_column, targets, slots):
    readers = tile_reader[:, 0]
    matches = (readers[:, None] == jnp.arange(targets, dtype=jnp.int32)[None, :]).astype(jnp.int32)
    ordinal = jnp.cumsum(matches, axis=0) - matches
    position = jnp.sum(ordinal * matches, axis=1)
    select = matches.T[:, None, :] * (
        position[None, None, :] == jnp.arange(slots, dtype=jnp.int32)[None, :, None]
    ).astype(jnp.int32)
    filled = jnp.sum(select, axis=2)
    local_index = jnp.sum(select * jnp.arange(readers.shape[0], dtype=jnp.int32)[None, None, :], axis=2)
    slot_position = jnp.sum(select * (tile_k * CT + tile_column)[None, None, :], axis=2) + filled - 1
    return filled, local_index, slot_position


def gather_kernel(nz, src_ref, amps_ref, residual_ref, out_ref, held, send_sem, recv_sem):
    zl = lax.axis_index("zl")
    c = lax.axis_index("core")
    b = lax.axis_index("bulk")
    partner = (zl, 1 - c, b)
    left = (zl - 1, c, b)
    right = (zl + 1, c, b)
    has_left = zl > 0
    has_right = zl < nz - 1
    own = zl * 2 + c

    barrier = pltpu.get_barrier_semaphore()
    pl.semaphore_signal(barrier, 1, device_id=partner, device_id_type=MESH)

    @pl.when(has_left)
    def _():
        pl.semaphore_signal(barrier, 1, device_id=left, device_id_type=MESH)

    @pl.when(has_right)
    def _():
        pl.semaphore_signal(barrier, 1, device_id=right, device_id_type=MESH)

    peers = 1 + has_left.astype(jnp.int32) + has_right.astype(jnp.int32)
    pl.semaphore_wait(barrier, peers)

    def copy(src, slot, kind, dev):
        return pltpu.make_async_remote_copy(
            src_ref=src,
            dst_ref=held.at[slot],
            send_sem=send_sem.at[slot, kind],
            recv_sem=recv_sem.at[slot],
            device_id=dev,
            device_id_type=MESH,
        )

    def accumulate(slot, block):
        out_ref[...] += jnp.dot(
            amps_ref[slot], block[...], precision=lax.Precision.HIGHEST,
            preferred_element_type=jnp.float32,
        )

    copy(src_ref, own, 0, partner).start()

    @pl.when(has_left)
    def _():
        copy(src_ref, own, 1, left).start()

    @pl.when(has_right)
    def _():
        copy(src_ref, own, 2, right).start()

    out_ref[...] = residual_ref[...]
    accumulate(own, src_ref)

    for d in range(1, nz):
        @pl.when(zl - d >= 0)
        def _():
            s = (zl - d) * 2 + c
            copy(held.at[s], s, 0, partner).wait_recv()
            copy(held.at[s], s, 0, partner).start()

            @pl.when(has_right)
            def _():
                copy(held.at[s], s, 2, right).start()

            accumulate(s, held.at[s])

        @pl.when(zl + d <= nz - 1)
        def _():
            s = (zl + d) * 2 + c
            copy(held.at[s], s, 0, partner).wait_recv()
            copy(held.at[s], s, 0, partner).start()

            @pl.when(has_left)
            def _():
                copy(held.at[s], s, 1, left).start()

            accumulate(s, held.at[s])

    for z in range(nz):
        s = z * 2 + (1 - c)
        copy(held.at[s], s, 0, partner).wait_recv()
        accumulate(s, held.at[s])

    for z in range(nz):
        s = z * 2 + c

        @pl.when(z == zl)
        def _():
            copy(src_ref, s, 0, partner).wait_send()

        @pl.when(z != zl)
        def _():
            copy(held.at[s], s, 0, partner).wait_send()

        @pl.when(has_left & (z == zl))
        def _():
            copy(src_ref, s, 1, left).wait_send()

        @pl.when(has_left & (z > zl))
        def _():
            copy(held.at[s], s, 1, left).wait_send()

        @pl.when(has_right & (z == zl))
        def _():
            copy(src_ref, s, 2, right).wait_send()

        @pl.when(has_right & (z < zl))
        def _():
            copy(held.at[s], s, 2, right).wait_send()


def gather_contract(placed, amps3, residual, nz):
    groups = 2 * nz
    return pl.pallas_call(
        functools.partial(gather_kernel, nz),
        out_shape=jax.ShapeDtypeStruct(residual.shape, jnp.float32),
        in_specs=[pl.BlockSpec(memory_space=pltpu.VMEM)] * 3,
        out_specs=pl.BlockSpec(memory_space=pltpu.VMEM),
        scratch_shapes=[
            pltpu.VMEM((groups,) + placed.shape, jnp.float32),
            pltpu.SemaphoreType.DMA((groups, 3)),
            pltpu.SemaphoreType.DMA((groups,)),
        ],
        compiler_params=pltpu.CompilerParams(
            collective_id=0, has_side_effects=True, vmem_limit_bytes=48 * 1024 * 1024
        ),
    )(placed, amps3, residual)


def exchange_kernel(nb, src_ref, out_ref, local_sem, send_sem, recv_sem):
    zl = lax.axis_index("zl")
    c = lax.axis_index("core")
    me = lax.axis_index("bulk")

    barrier = pltpu.get_barrier_semaphore()

    def greet(p, carry):
        pl.semaphore_signal(barrier, 1, device_id=(zl, c, lax.rem(me + p, nb)), device_id_type=MESH)
        return carry

    lax.fori_loop(1, nb, greet, 0)
    pl.semaphore_wait(barrier, nb - 1)

    mine = pltpu.make_async_copy(src_ref.at[me], out_ref.at[me], local_sem)
    mine.start()

    def copy(p, dest):
        return pltpu.make_async_remote_copy(
            src_ref=src_ref.at[dest],
            dst_ref=out_ref.at[me],
            send_sem=send_sem.at[p],
            recv_sem=recv_sem.at[me],
            device_id=(zl, c, dest),
            device_id_type=MESH,
        )

    def send(p, carry):
        copy(p, lax.rem(me + p, nb)).start()
        return carry

    lax.fori_loop(1, nb, send, 0)

    def receive(p, carry):
        source = lax.rem(me + nb - p, nb)
        pltpu.make_async_remote_copy(
            src_ref=src_ref.at[source],
            dst_ref=out_ref.at[source],
            send_sem=send_sem.at[p],
            recv_sem=recv_sem.at[source],
            device_id=(zl, c, source),
            device_id_type=MESH,
        ).wait_recv()
        return carry

    lax.fori_loop(1, nb, receive, 0)
    mine.wait()

    def sent(p, carry):
        copy(p, lax.rem(me + p, nb)).wait_send()
        return carry

    lax.fori_loop(1, nb, sent, 0)


def bulk_exchange(outgoing, nb):
    return pl.pallas_call(
        functools.partial(exchange_kernel, nb),
        out_shape=jax.ShapeDtypeStruct(outgoing.shape, outgoing.dtype),
        in_specs=[pl.BlockSpec(memory_space=pltpu.VMEM)],
        out_specs=pl.BlockSpec(memory_space=pltpu.VMEM),
        scratch_shapes=[
            pltpu.SemaphoreType.DMA(()),
            pltpu.SemaphoreType.DMA((nb,)),
            pltpu.SemaphoreType.DMA((nb,)),
        ],
        compiler_params=pltpu.CompilerParams(collective_id=1, has_side_effects=True),
    )(outgoing)


def local(residual_in, amplitudes, integral_tiles, tile_reader, tile_k, tile_column):
    targets = lax.axis_size("bulk")
    height, width = integral_tiles.shape[1], integral_tiles.shape[2]
    filled, local_index, slot_position = bucket_slots(
        tile_reader, tile_k, tile_column, targets, SLOT
    )
    picked = jnp.take(integral_tiles, local_index.reshape(-1), axis=0)
    picked = jnp.where(filled.reshape(-1)[:, None, None] > 0, picked, 0.0)
    rows, own_cols = amplitudes.shape
    label = jnp.zeros((targets, 1, width), jnp.float32).at[:, 0, :SLOT].set(
        slot_position.reshape(targets, SLOT).astype(jnp.float32)
    )
    amp_rows = rows * own_cols // width
    amp_block = jnp.broadcast_to(amplitudes.reshape(1, amp_rows, width), (targets, amp_rows, width))
    outgoing = jnp.concatenate(
        [picked.reshape(targets, SLOT * height, width), label, amp_block], axis=1
    )
    arrived = bulk_exchange(outgoing, targets)
    position = arrived[:, SLOT * height, :SLOT].reshape(-1).astype(jnp.int32)
    amps = arrived[:, SLOT * height + 1 :, :].reshape(targets, rows, own_cols)
    amps = amps.transpose(1, 0, 2).reshape(rows, targets * own_cols)
    arrived = arrived[:, : SLOT * height, :].reshape(targets * SLOT, height * width)
    table = (position[None, :] == jnp.arange(KT * CT, dtype=jnp.int32)[:, None]).astype(jnp.float32)
    placed = jnp.dot(table, arrived, precision=lax.Precision.HIGHEST)
    placed = placed.reshape(KT, CT, height, width).transpose(0, 2, 1, 3).reshape(KT * height, CT * width)
    nz = lax.axis_size("zl")
    groups = 2 * nz
    amps3 = amps.reshape(rows, KT, groups, height).transpose(2, 0, 1, 3).reshape(groups, rows, KT * height)
    return gather_contract(placed, amps3, residual_in, nz)


def solution(mesh):
    row_size = mesh.shape["row"]
    devices = np.asarray(mesh.devices).reshape(row_size // 2, 2, mesh.shape["bulk"])
    inner = Mesh(devices, ("zl", "core", "bulk"))
    row = ("zl", "core")
    placed = (
        P(row, "bulk"),
        P(row, "bulk"),
        P("bulk", row, None),
        P("bulk", None),
        P("bulk"),
        P("bulk"),
    )
    return jax.shard_map(
        local, mesh=inner, in_specs=placed, out_specs=P(row, "bulk"), check_vma=False
    )
```

```python
import functools

import jax
import jax.numpy as jnp
import numpy as np
from jax import lax
from jax.experimental import pallas as pl
from jax.experimental.pallas import tpu as pltpu
from jax.sharding import Mesh, PartitionSpec as P

MESH = pl.DeviceIdType.MESH

KT = 16
CT = 8
SLOT = 2


def bucket_slots(tile_reader, tile_k, tile_column, targets, slots):
    readers = tile_reader[:, 0]
    matches = (readers[:, None] == jnp.arange(targets, dtype=jnp.int32)[None, :]).astype(jnp.int32)
    ordinal = jnp.cumsum(matches, axis=0) - matches
    position = jnp.sum(ordinal * matches, axis=1)
    select = matches.T[:, None, :] * (
        position[None, None, :] == jnp.arange(slots, dtype=jnp.int32)[None, :, None]
    ).astype(jnp.int32)
    filled = jnp.sum(select, axis=2)
    local_index = jnp.sum(select * jnp.arange(readers.shape[0], dtype=jnp.int32)[None, None, :], axis=2)
    slot_position = jnp.sum(select * (tile_k * CT + tile_column)[None, None, :], axis=2) + filled - 1
    return filled, local_index, slot_position


def contract_kernel(nz, nb, src_ref, mine_ref, residual_ref, out_ref, held, amps_buf,
                    send_sem, recv_sem, amp_send, amp_recv):
    zl = lax.axis_index("zl")
    c = lax.axis_index("core")
    me = lax.axis_index("bulk")
    partner = (zl, 1 - c, me)
    left = (zl - 1, c, me)
    right = (zl + 1, c, me)
    has_left = zl > 0
    has_right = zl < nz - 1
    own = zl * 2 + c
    n_m = amps_buf.shape[0]

    barrier = pltpu.get_barrier_semaphore()
    pl.semaphore_signal(barrier, 1, device_id=partner, device_id_type=MESH)

    @pl.when(has_left)
    def _():
        pl.semaphore_signal(barrier, 1, device_id=left, device_id_type=MESH)

    @pl.when(has_right)
    def _():
        pl.semaphore_signal(barrier, 1, device_id=right, device_id_type=MESH)

    def greet(p, carry):
        pl.semaphore_signal(barrier, 1, device_id=(zl, c, lax.rem(me + p, nb)), device_id_type=MESH)
        return carry

    lax.fori_loop(1, nb, greet, 0)
    peers = nb + has_left.astype(jnp.int32) + has_right.astype(jnp.int32)
    pl.semaphore_wait(barrier, peers)

    my_m = lax.rem(me, n_m)
    my_k = me // n_m

    def amp_copy(p, dest):
        return pltpu.make_async_remote_copy(
            src_ref=mine_ref,
            dst_ref=amps_buf.at[my_m, my_k],
            send_sem=amp_send.at[p],
            recv_sem=amp_recv.at[me],
            device_id=(zl, c, dest),
            device_id_type=MESH,
        )

    def amp_send_one(p, carry):
        amp_copy(p, lax.rem(me + p, nb)).start()
        return carry

    lax.fori_loop(1, nb, amp_send_one, 0)
    amps_buf[my_m, my_k] = mine_ref[...]

    def copy(src, slot, kind, dev):
        return pltpu.make_async_remote_copy(
            src_ref=src,
            dst_ref=held.at[slot],
            send_sem=send_sem.at[slot, kind],
            recv_sem=recv_sem.at[slot],
            device_id=dev,
            device_id_type=MESH,
        )

    copy(src_ref, own, 0, partner).start()

    @pl.when(has_left)
    def _():
        copy(src_ref, own, 1, left).start()

    @pl.when(has_right)
    def _():
        copy(src_ref, own, 2, right).start()

    def amp_wait(p, carry):
        source = lax.rem(me + nb - p, nb)
        pltpu.make_async_remote_copy(
            src_ref=mine_ref,
            dst_ref=amps_buf.at[lax.rem(source, n_m), source // n_m],
            send_sem=amp_send.at[p],
            recv_sem=amp_recv.at[source],
            device_id=(zl, c, source),
            device_id_type=MESH,
        ).wait_recv()
        return carry

    def accumulate(slot, block):
        half = held.shape[1] // amps_buf.shape[1]
        part = amps_buf[slot // 2, :, pl.ds(lax.rem(slot, 2) * half, half), :]
        lhs_t = part.reshape(-1, part.shape[-1])
        out_ref[...] += jnp.dot(
            lhs_t.T, block[...], precision=lax.Precision.HIGHEST,
            preferred_element_type=jnp.float32,
        )

    for d in range(1, nz):
        @pl.when(zl - d >= 0)
        def _():
            s = (zl - d) * 2 + c
            copy(held.at[s], s, 0, partner).wait_recv()
            copy(held.at[s], s, 0, partner).start()

            @pl.when(has_right)
            def _():
                copy(held.at[s], s, 2, right).start()

        @pl.when(zl + d <= nz - 1)
        def _():
            s = (zl + d) * 2 + c
            copy(held.at[s], s, 0, partner).wait_recv()
            copy(held.at[s], s, 0, partner).start()

            @pl.when(has_left)
            def _():
                copy(held.at[s], s, 1, left).start()

    lax.fori_loop(1, nb, amp_wait, 0)
    out_ref[...] = residual_ref[...]
    accumulate(own, src_ref)
    for z in range(nz):
        s = z * 2 + c

        @pl.when(z != zl)
        def _():
            accumulate(s, held.at[s])

    for z in range(nz):
        s = z * 2 + (1 - c)
        copy(held.at[s], s, 0, partner).wait_recv()
        accumulate(s, held.at[s])

    for z in range(nz):
        s = z * 2 + c

        @pl.when(z == zl)
        def _():
            copy(src_ref, s, 0, partner).wait_send()

        @pl.when(z != zl)
        def _():
            copy(held.at[s], s, 0, partner).wait_send()

        @pl.when(has_left & (z == zl))
        def _():
            copy(src_ref, s, 1, left).wait_send()

        @pl.when(has_left & (z > zl))
        def _():
            copy(held.at[s], s, 1, left).wait_send()

        @pl.when(has_right & (z == zl))
        def _():
            copy(src_ref, s, 2, right).wait_send()

        @pl.when(has_right & (z < zl))
        def _():
            copy(held.at[s], s, 2, right).wait_send()

    def amp_sent(p, carry):
        amp_copy(p, lax.rem(me + p, nb)).wait_send()
        return carry

    lax.fori_loop(1, nb, amp_sent, 0)


def gather_contract(placed, mine_t, residual, nz, nb, n_m):
    groups = 2 * nz
    n_k = nb // n_m
    return pl.pallas_call(
        functools.partial(contract_kernel, nz, nb),
        out_shape=jax.ShapeDtypeStruct(residual.shape, jnp.float32),
        in_specs=[pl.BlockSpec(memory_space=pltpu.VMEM)] * 3,
        out_specs=pl.BlockSpec(memory_space=pltpu.VMEM),
        scratch_shapes=[
            pltpu.VMEM((groups,) + placed.shape, jnp.float32),
            pltpu.VMEM((n_m, n_k) + mine_t.shape, jnp.float32),
            pltpu.SemaphoreType.DMA((groups, 3)),
            pltpu.SemaphoreType.DMA((groups,)),
            pltpu.SemaphoreType.DMA((nb,)),
            pltpu.SemaphoreType.DMA((nb,)),
        ],
        compiler_params=pltpu.CompilerParams(
            collective_id=0, has_side_effects=True, vmem_limit_bytes=48 * 1024 * 1024
        ),
    )(placed, mine_t, residual)


def exchange_kernel(nb, src_ref, out_ref, local_sem, send_sem, recv_sem):
    zl = lax.axis_index("zl")
    c = lax.axis_index("core")
    me = lax.axis_index("bulk")

    barrier = pltpu.get_barrier_semaphore()

    def greet(p, carry):
        pl.semaphore_signal(barrier, 1, device_id=(zl, c, lax.rem(me + p, nb)), device_id_type=MESH)
        return carry

    lax.fori_loop(1, nb, greet, 0)
    pl.semaphore_wait(barrier, nb - 1)

    mine = pltpu.make_async_copy(src_ref.at[me], out_ref.at[me], local_sem)
    mine.start()

    def copy(p, dest):
        return pltpu.make_async_remote_copy(
            src_ref=src_ref.at[dest],
            dst_ref=out_ref.at[me],
            send_sem=send_sem.at[p],
            recv_sem=recv_sem.at[me],
            device_id=(zl, c, dest),
            device_id_type=MESH,
        )

    def send(p, carry):
        copy(p, lax.rem(me + p, nb)).start()
        return carry

    lax.fori_loop(1, nb, send, 0)

    def receive(p, carry):
        source = lax.rem(me + nb - p, nb)
        pltpu.make_async_remote_copy(
            src_ref=src_ref.at[source],
            dst_ref=out_ref.at[source],
            send_sem=send_sem.at[p],
            recv_sem=recv_sem.at[source],
            device_id=(zl, c, source),
            device_id_type=MESH,
        ).wait_recv()
        return carry

    lax.fori_loop(1, nb, receive, 0)
    mine.wait()

    def sent(p, carry):
        copy(p, lax.rem(me + p, nb)).wait_send()
        return carry

    lax.fori_loop(1, nb, sent, 0)


def bulk_exchange(outgoing, nb):
    return pl.pallas_call(
        functools.partial(exchange_kernel, nb),
        out_shape=jax.ShapeDtypeStruct(outgoing.shape, outgoing.dtype),
        in_specs=[pl.BlockSpec(memory_space=pltpu.VMEM)],
        out_specs=pl.BlockSpec(memory_space=pltpu.VMEM),
        scratch_shapes=[
            pltpu.SemaphoreType.DMA(()),
            pltpu.SemaphoreType.DMA((nb,)),
            pltpu.SemaphoreType.DMA((nb,)),
        ],
        compiler_params=pltpu.CompilerParams(collective_id=1, has_side_effects=True),
    )(outgoing)


def local(residual_in, amplitudes, integral_tiles, tile_reader, tile_k, tile_column):
    targets = lax.axis_size("bulk")
    height, width = integral_tiles.shape[1], integral_tiles.shape[2]
    filled, local_index, slot_position = bucket_slots(
        tile_reader, tile_k, tile_column, targets, SLOT
    )
    picked = jnp.take(integral_tiles, local_index.reshape(-1), axis=0)
    picked = jnp.where(filled.reshape(-1)[:, None, None] > 0, picked, 0.0)
    label = jnp.zeros((targets, 1, width), jnp.float32).at[:, 0, :SLOT].set(
        slot_position.reshape(targets, SLOT).astype(jnp.float32)
    )
    outgoing = jnp.concatenate([picked.reshape(targets, SLOT * height, width), label], axis=1)
    arrived = bulk_exchange(outgoing, targets)
    position = arrived[:, SLOT * height, :SLOT].reshape(-1).astype(jnp.int32)
    arrived = arrived[:, : SLOT * height, :].reshape(targets * SLOT, height * width)
    table = (position[None, :] == jnp.arange(KT * CT, dtype=jnp.int32)[:, None]).astype(jnp.float32)
    placed = jnp.dot(table, arrived, precision=lax.Precision.HIGHEST)
    placed = placed.reshape(KT, CT, height, width).transpose(0, 2, 1, 3).reshape(KT * height, CT * width)
    nz = lax.axis_size("zl")
    rows, own_cols = amplitudes.shape
    return gather_contract(placed, amplitudes.T, residual_in, nz, targets, width // own_cols)


def solution(mesh):
    row_size = mesh.shape["row"]
    devices = np.asarray(mesh.devices).reshape(row_size // 2, 2, mesh.shape["bulk"])
    inner = Mesh(devices, ("zl", "core", "bulk"))
    row = ("zl", "core")
    placed = (
        P(row, "bulk"),
        P(row, "bulk"),
        P("bulk", row, None),
        P("bulk", None),
        P("bulk"),
        P("bulk"),
    )
    return jax.shard_map(
        local, mesh=inner, in_specs=placed, out_specs=P(row, "bulk"), check_vma=False
    )
```

```python
import functools

import jax
import jax.numpy as jnp
import numpy as np
from jax import lax
from jax.experimental import pallas as pl
from jax.experimental.pallas import tpu as pltpu
from jax.sharding import Mesh, PartitionSpec as P

MESH = pl.DeviceIdType.MESH

KT = 16
CT = 8
SLOT = 2


def bucket_slots(tile_reader, tile_k, tile_column, targets, slots):
    readers = tile_reader[:, 0]
    matches = (readers[:, None] == jnp.arange(targets, dtype=jnp.int32)[None, :]).astype(jnp.int32)
    ordinal = jnp.cumsum(matches, axis=0) - matches
    position = jnp.sum(ordinal * matches, axis=1)
    select = matches.T[:, None, :] * (
        position[None, None, :] == jnp.arange(slots, dtype=jnp.int32)[None, :, None]
    ).astype(jnp.int32)
    filled = jnp.sum(select, axis=2)
    local_index = jnp.sum(select * jnp.arange(readers.shape[0], dtype=jnp.int32)[None, None, :], axis=2)
    slot_position = jnp.sum(select * (tile_k * CT + tile_column)[None, None, :], axis=2) + filled - 1
    return filled, local_index, slot_position


def contract_kernel(nz, nb, src_ref, mine_ref, cross_ref, residual_ref, out_ref, held, amps_buf,
                    send_sem, recv_sem, amp_send, amp_recv):
    zl = lax.axis_index("zl")
    c = lax.axis_index("core")
    me = lax.axis_index("bulk")
    partner = (zl, 1 - c, me)
    left = (zl - 1, c, me)
    right = (zl + 1, c, me)
    has_left = zl > 0
    has_right = zl < nz - 1
    own = zl * 2 + c
    n_m = amps_buf.shape[0]
    half = nb // 2
    side = me // half
    me_in = lax.rem(me, half)

    barrier = pltpu.get_barrier_semaphore()
    pl.semaphore_signal(barrier, 1, device_id=partner, device_id_type=MESH)

    @pl.when(has_left)
    def _():
        pl.semaphore_signal(barrier, 1, device_id=left, device_id_type=MESH)

    @pl.when(has_right)
    def _():
        pl.semaphore_signal(barrier, 1, device_id=right, device_id_type=MESH)

    def near(q):
        return side * half + lax.rem(me_in + q, half)

    def greet(q, carry):
        pl.semaphore_signal(barrier, 1, device_id=(zl, c, near(q)), device_id_type=MESH)
        return carry

    lax.fori_loop(1, half, greet, 0)
    peers = half + has_left.astype(jnp.int32) + has_right.astype(jnp.int32)
    pl.semaphore_wait(barrier, peers)

    my_m = lax.rem(me, n_m)
    my_k = me // n_m

    def amp_copy(p, dest):
        return pltpu.make_async_remote_copy(
            src_ref=mine_ref,
            dst_ref=amps_buf.at[my_m, my_k],
            send_sem=amp_send.at[p],
            recv_sem=amp_recv.at[me],
            device_id=(zl, c, dest),
            device_id_type=MESH,
        )

    def amp_send_one(q, carry):
        amp_copy(q, near(q)).start()
        return carry

    lax.fori_loop(1, half, amp_send_one, 0)
    amps_buf[my_m, my_k] = mine_ref[...]

    def copy(src, slot, kind, dev):
        return pltpu.make_async_remote_copy(
            src_ref=src,
            dst_ref=held.at[slot],
            send_sem=send_sem.at[slot, kind],
            recv_sem=recv_sem.at[slot],
            device_id=dev,
            device_id_type=MESH,
        )

    copy(src_ref, own, 0, partner).start()

    @pl.when(has_left)
    def _():
        copy(src_ref, own, 1, left).start()

    @pl.when(has_right)
    def _():
        copy(src_ref, own, 2, right).start()

    def amp_wait(q, carry):
        source = near(half - q)
        pltpu.make_async_remote_copy(
            src_ref=mine_ref,
            dst_ref=amps_buf.at[lax.rem(source, n_m), source // n_m],
            send_sem=amp_send.at[q],
            recv_sem=amp_recv.at[source],
            device_id=(zl, c, source),
            device_id_type=MESH,
        ).wait_recv()
        return carry

    def accumulate(slot, block):
        rows_k = held.shape[1] // amps_buf.shape[1]
        window = pl.ds(lax.rem(slot, 2) * rows_k, rows_k)
        near_part = amps_buf[slot // 2, :, window, :]
        far_part = cross_ref[slot // 2, :, window, :]
        n_k = amps_buf.shape[1]
        k_side = lax.broadcasted_iota(jnp.int32, near_part.shape, 0) // (n_k // 2)
        part = jnp.where(k_side == side, near_part, far_part)
        lhs_t = part.reshape(-1, part.shape[-1])
        out_ref[...] += jnp.dot(
            lhs_t.T, block[...], precision=lax.Precision.HIGHEST,
            preferred_element_type=jnp.float32,
        )

    for d in range(1, nz):
        @pl.when(zl - d >= 0)
        def _():
            s = (zl - d) * 2 + c
            copy(held.at[s], s, 0, partner).wait_recv()
            copy(held.at[s], s, 0, partner).start()

            @pl.when(has_right)
            def _():
                copy(held.at[s], s, 2, right).start()

        @pl.when(zl + d <= nz - 1)
        def _():
            s = (zl + d) * 2 + c
            copy(held.at[s], s, 0, partner).wait_recv()
            copy(held.at[s], s, 0, partner).start()

            @pl.when(has_left)
            def _():
                copy(held.at[s], s, 1, left).start()

    lax.fori_loop(1, half, amp_wait, 0)
    out_ref[...] = residual_ref[...]
    accumulate(own, src_ref)
    for z in range(nz):
        s = z * 2 + c

        @pl.when(z != zl)
        def _():
            accumulate(s, held.at[s])

    for z in range(nz):
        s = z * 2 + (1 - c)
        copy(held.at[s], s, 0, partner).wait_recv()
        accumulate(s, held.at[s])

    for z in range(nz):
        s = z * 2 + c

        @pl.when(z == zl)
        def _():
            copy(src_ref, s, 0, partner).wait_send()

        @pl.when(z != zl)
        def _():
            copy(held.at[s], s, 0, partner).wait_send()

        @pl.when(has_left & (z == zl))
        def _():
            copy(src_ref, s, 1, left).wait_send()

        @pl.when(has_left & (z > zl))
        def _():
            copy(held.at[s], s, 1, left).wait_send()

        @pl.when(has_right & (z == zl))
        def _():
            copy(src_ref, s, 2, right).wait_send()

        @pl.when(has_right & (z < zl))
        def _():
            copy(held.at[s], s, 2, right).wait_send()

    def amp_sent(q, carry):
        amp_copy(q, near(q)).wait_send()
        return carry

    lax.fori_loop(1, half, amp_sent, 0)


def gather_contract(placed, mine_t, cross, residual, nz, nb, n_m):
    groups = 2 * nz
    n_k = nb // n_m
    return pl.pallas_call(
        functools.partial(contract_kernel, nz, nb),
        out_shape=jax.ShapeDtypeStruct(residual.shape, jnp.float32),
        in_specs=[pl.BlockSpec(memory_space=pltpu.VMEM)] * 4,
        out_specs=pl.BlockSpec(memory_space=pltpu.VMEM),
        scratch_shapes=[
            pltpu.VMEM((groups,) + placed.shape, jnp.float32),
            pltpu.VMEM((n_m, n_k) + mine_t.shape, jnp.float32),
            pltpu.SemaphoreType.DMA((groups, 3)),
            pltpu.SemaphoreType.DMA((groups,)),
            pltpu.SemaphoreType.DMA((nb,)),
            pltpu.SemaphoreType.DMA((nb,)),
        ],
        compiler_params=pltpu.CompilerParams(
            collective_id=0, has_side_effects=True, vmem_limit_bytes=48 * 1024 * 1024
        ),
    )(placed, mine_t, cross, residual)


def exchange_kernel(nb, n_m, src_ref, mine_ref, out_ref, cross_ref, local_sem, send_sem, recv_sem,
                    amp_send, amp_recv):
    zl = lax.axis_index("zl")
    c = lax.axis_index("core")
    me = lax.axis_index("bulk")

    half = nb // 2
    far_side = 1 - me // half
    me_in = lax.rem(me, half)
    my_m = lax.rem(me, n_m)
    my_k = me // n_m
    cross_ref[...] = jnp.zeros_like(cross_ref)
    barrier = pltpu.get_barrier_semaphore()

    def greet(p, carry):
        pl.semaphore_signal(barrier, 1, device_id=(zl, c, lax.rem(me + p, nb)), device_id_type=MESH)
        return carry

    lax.fori_loop(1, nb, greet, 0)
    pl.semaphore_wait(barrier, nb - 1)

    mine = pltpu.make_async_copy(src_ref.at[me], out_ref.at[me], local_sem)
    mine.start()

    def copy(p, dest):
        return pltpu.make_async_remote_copy(
            src_ref=src_ref.at[dest],
            dst_ref=out_ref.at[me],
            send_sem=send_sem.at[p],
            recv_sem=recv_sem.at[me],
            device_id=(zl, c, dest),
            device_id_type=MESH,
        )

    def send(p, carry):
        copy(p, lax.rem(me + p, nb)).start()
        return carry

    lax.fori_loop(1, nb, send, 0)

    def far(q):
        return far_side * half + lax.rem(me_in + q, half)

    def amp_copy(q, dest):
        return pltpu.make_async_remote_copy(
            src_ref=mine_ref,
            dst_ref=cross_ref.at[my_m, my_k],
            send_sem=amp_send.at[q],
            recv_sem=amp_recv.at[me],
            device_id=(zl, c, dest),
            device_id_type=MESH,
        )

    def amp_send_one(q, carry):
        amp_copy(q, far(q)).start()
        return carry

    lax.fori_loop(0, half, amp_send_one, 0)

    def receive(p, carry):
        source = lax.rem(me + nb - p, nb)
        pltpu.make_async_remote_copy(
            src_ref=src_ref.at[source],
            dst_ref=out_ref.at[source],
            send_sem=send_sem.at[p],
            recv_sem=recv_sem.at[source],
            device_id=(zl, c, source),
            device_id_type=MESH,
        ).wait_recv()
        return carry

    lax.fori_loop(1, nb, receive, 0)
    mine.wait()

    def amp_wait(q, carry):
        source = far(half - q)
        pltpu.make_async_remote_copy(
            src_ref=mine_ref,
            dst_ref=cross_ref.at[lax.rem(source, n_m), source // n_m],
            send_sem=amp_send.at[q],
            recv_sem=amp_recv.at[source],
            device_id=(zl, c, source),
            device_id_type=MESH,
        ).wait_recv()
        return carry

    lax.fori_loop(0, half, amp_wait, 0)

    def amp_sent(q, carry):
        amp_copy(q, far(q)).wait_send()
        return carry

    lax.fori_loop(0, half, amp_sent, 0)

    def sent(p, carry):
        copy(p, lax.rem(me + p, nb)).wait_send()
        return carry

    lax.fori_loop(1, nb, sent, 0)


def bulk_exchange(outgoing, mine_t, nb, n_m):
    return pl.pallas_call(
        functools.partial(exchange_kernel, nb, n_m),
        out_shape=(
            jax.ShapeDtypeStruct(outgoing.shape, outgoing.dtype),
            jax.ShapeDtypeStruct((n_m, nb // n_m) + mine_t.shape, jnp.float32),
        ),
        in_specs=[pl.BlockSpec(memory_space=pltpu.VMEM)] * 2,
        out_specs=(pl.BlockSpec(memory_space=pltpu.VMEM), pl.BlockSpec(memory_space=pltpu.VMEM)),
        scratch_shapes=[
            pltpu.SemaphoreType.DMA(()),
            pltpu.SemaphoreType.DMA((nb,)),
            pltpu.SemaphoreType.DMA((nb,)),
            pltpu.SemaphoreType.DMA((nb,)),
            pltpu.SemaphoreType.DMA((nb,)),
        ],
        compiler_params=pltpu.CompilerParams(collective_id=1, has_side_effects=True),
    )(outgoing, mine_t)


def local(residual_in, amplitudes, integral_tiles, tile_reader, tile_k, tile_column):
    targets = lax.axis_size("bulk")
    height, width = integral_tiles.shape[1], integral_tiles.shape[2]
    filled, local_index, slot_position = bucket_slots(
        tile_reader, tile_k, tile_column, targets, SLOT
    )
    picked = jnp.take(integral_tiles, local_index.reshape(-1), axis=0)
    picked = jnp.where(filled.reshape(-1)[:, None, None] > 0, picked, 0.0)
    label = jnp.zeros((targets, 1, width), jnp.float32).at[:, 0, :SLOT].set(
        slot_position.reshape(targets, SLOT).astype(jnp.float32)
    )
    outgoing = jnp.concatenate([picked.reshape(targets, SLOT * height, width), label], axis=1)
    rows, own_cols = amplitudes.shape
    n_m = width // own_cols
    mine_t = amplitudes.T
    arrived, cross = bulk_exchange(outgoing, mine_t, targets, n_m)
    position = arrived[:, SLOT * height, :SLOT].reshape(-1).astype(jnp.int32)
    arrived = arrived[:, : SLOT * height, :].reshape(targets * SLOT, height * width)
    table = (position[None, :] == jnp.arange(KT * CT, dtype=jnp.int32)[:, None]).astype(jnp.float32)
    placed = jnp.dot(table, arrived, precision=lax.Precision.HIGHEST)
    placed = placed.reshape(KT, CT, height, width).transpose(0, 2, 1, 3).reshape(KT * height, CT * width)
    nz = lax.axis_size("zl")
    return gather_contract(placed, mine_t, cross, residual_in, nz, targets, n_m)


def solution(mesh):
    row_size = mesh.shape["row"]
    devices = np.asarray(mesh.devices).reshape(row_size // 2, 2, mesh.shape["bulk"])
    inner = Mesh(devices, ("zl", "core", "bulk"))
    row = ("zl", "core")
    placed = (
        P(row, "bulk"),
        P(row, "bulk"),
        P("bulk", row, None),
        P("bulk", None),
        P("bulk"),
        P("bulk"),
    )
    return jax.shard_map(
        local, mesh=inner, in_specs=placed, out_specs=P(row, "bulk"), check_vma=False
    )
```

```python
import functools

import jax
import jax.numpy as jnp
import numpy as np
from jax import lax
from jax.experimental import pallas as pl
from jax.experimental.pallas import tpu as pltpu
from jax.sharding import Mesh, PartitionSpec as P

MESH = pl.DeviceIdType.MESH

KT = 16
CT = 8
SLOT = 2
Z_HALVES = 2


def bucket_slots(tile_reader, tile_k, tile_column, targets, slots):
    readers = tile_reader[:, 0]
    matches = (readers[:, None] == jnp.arange(targets, dtype=jnp.int32)[None, :]).astype(jnp.int32)
    ordinal = jnp.cumsum(matches, axis=0) - matches
    position = jnp.sum(ordinal * matches, axis=1)
    select = matches.T[:, None, :] * (
        position[None, None, :] == jnp.arange(slots, dtype=jnp.int32)[None, :, None]
    ).astype(jnp.int32)
    filled = jnp.sum(select, axis=2)
    local_index = jnp.sum(select * jnp.arange(readers.shape[0], dtype=jnp.int32)[None, None, :], axis=2)
    slot_position = jnp.sum(select * (tile_k * CT + tile_column)[None, None, :], axis=2) + filled - 1
    return filled, local_index, slot_position


def gather_kernel(nz, src_ref, out_ref, local_sem, send_sem, recv_sem):
    zl = lax.axis_index("zl")
    c = lax.axis_index("core")
    zh = lax.axis_index("zh")
    xy = lax.axis_index("xy")
    partner = (zl, 1 - c, zh, xy)
    left = (zl - 1, c, zh, xy)
    right = (zl + 1, c, zh, xy)
    has_left = zl > 0
    has_right = zl < nz - 1
    own = zl * 2 + c

    barrier = pltpu.get_barrier_semaphore()
    pl.semaphore_signal(barrier, 1, device_id=partner, device_id_type=MESH)

    @pl.when(has_left)
    def _():
        pl.semaphore_signal(barrier, 1, device_id=left, device_id_type=MESH)

    @pl.when(has_right)
    def _():
        pl.semaphore_signal(barrier, 1, device_id=right, device_id_type=MESH)

    peers = 1 + has_left.astype(jnp.int32) + has_right.astype(jnp.int32)
    pl.semaphore_wait(barrier, peers)

    def copy(src, slot, kind, dev):
        return pltpu.make_async_remote_copy(
            src_ref=src,
            dst_ref=out_ref.at[slot],
            send_sem=send_sem.at[slot, kind],
            recv_sem=recv_sem.at[slot],
            device_id=dev,
            device_id_type=MESH,
        )

    mine = pltpu.make_async_copy(src_ref, out_ref.at[own], local_sem)
    mine.start()
    copy(src_ref, own, 0, partner).start()

    @pl.when(has_left)
    def _():
        copy(src_ref, own, 1, left).start()

    @pl.when(has_right)
    def _():
        copy(src_ref, own, 2, right).start()

    for d in range(1, nz):
        @pl.when(zl - d >= 0)
        def _():
            s = (zl - d) * 2 + c
            copy(out_ref.at[s], s, 0, partner).wait_recv()
            copy(out_ref.at[s], s, 0, partner).start()

            @pl.when(has_right)
            def _():
                copy(out_ref.at[s], s, 2, right).start()

        @pl.when(zl + d <= nz - 1)
        def _():
            s = (zl + d) * 2 + c
            copy(out_ref.at[s], s, 0, partner).wait_recv()
            copy(out_ref.at[s], s, 0, partner).start()

            @pl.when(has_left)
            def _():
                copy(out_ref.at[s], s, 1, left).start()

    for z in range(nz):
        s = z * 2 + (1 - c)
        copy(out_ref.at[s], s, 0, partner).wait_recv()

    mine.wait()
    for z in range(nz):
        s = z * 2 + c
        copy(out_ref.at[s], s, 0, partner).wait_send()

        @pl.when(has_left & (z >= zl))
        def _():
            copy(out_ref.at[s], s, 1, left).wait_send()

        @pl.when(has_right & (z <= zl))
        def _():
            copy(out_ref.at[s], s, 2, right).wait_send()


def row_gather(placed, nz):
    groups = 2 * nz
    return pl.pallas_call(
        functools.partial(gather_kernel, nz),
        out_shape=jax.ShapeDtypeStruct((groups,) + placed.shape, placed.dtype),
        in_specs=[pl.BlockSpec(memory_space=pltpu.VMEM)],
        out_specs=pl.BlockSpec(memory_space=pltpu.VMEM),
        scratch_shapes=[
            pltpu.SemaphoreType.DMA(()),
            pltpu.SemaphoreType.DMA((groups, 3)),
            pltpu.SemaphoreType.DMA((groups,)),
        ],
        compiler_params=pltpu.CompilerParams(collective_id=0, has_side_effects=True),
    )(placed)


def exchange_kernel(nb, nxy, src_ref, out_ref, local_sem, send_sem, recv_sem):
    zl = lax.axis_index("zl")
    c = lax.axis_index("core")
    me = lax.axis_index("zh") * nxy + lax.axis_index("xy")

    def peer(b):
        return (zl, c, b // nxy, lax.rem(b, nxy))

    barrier = pltpu.get_barrier_semaphore()

    def greet(p, carry):
        pl.semaphore_signal(barrier, 1, device_id=peer(lax.rem(me + p, nb)), device_id_type=MESH)
        return carry

    lax.fori_loop(1, nb, greet, 0)
    pl.semaphore_wait(barrier, nb - 1)

    mine = pltpu.make_async_copy(src_ref.at[me], out_ref.at[me], local_sem)
    mine.start()

    def copy(p, dest):
        return pltpu.make_async_remote_copy(
            src_ref=src_ref.at[dest],
            dst_ref=out_ref.at[me],
            send_sem=send_sem.at[p],
            recv_sem=recv_sem.at[me],
            device_id=peer(dest),
            device_id_type=MESH,
        )

    def send(p, carry):
        copy(p, lax.rem(me + p, nb)).start()
        return carry

    lax.fori_loop(1, nb, send, 0)

    def receive(p, carry):
        source = lax.rem(me + nb - p, nb)
        pltpu.make_async_remote_copy(
            src_ref=src_ref.at[source],
            dst_ref=out_ref.at[source],
            send_sem=send_sem.at[p],
            recv_sem=recv_sem.at[source],
            device_id=peer(source),
            device_id_type=MESH,
        ).wait_recv()
        return carry

    lax.fori_loop(1, nb, receive, 0)
    mine.wait()

    def sent(p, carry):
        copy(p, lax.rem(me + p, nb)).wait_send()
        return carry

    lax.fori_loop(1, nb, sent, 0)


def bulk_exchange(outgoing, nb, nxy):
    return pl.pallas_call(
        functools.partial(exchange_kernel, nb, nxy),
        out_shape=jax.ShapeDtypeStruct(outgoing.shape, outgoing.dtype),
        in_specs=[pl.BlockSpec(memory_space=pltpu.VMEM)],
        out_specs=pl.BlockSpec(memory_space=pltpu.VMEM),
        scratch_shapes=[
            pltpu.SemaphoreType.DMA(()),
            pltpu.SemaphoreType.DMA((nb,)),
            pltpu.SemaphoreType.DMA((nb,)),
        ],
        compiler_params=pltpu.CompilerParams(collective_id=1, has_side_effects=True),
    )(outgoing)


def local(residual_in, amplitudes, integral_tiles, tile_reader, tile_k, tile_column):
    nxy = lax.axis_size("xy")
    targets = lax.axis_size("zh") * nxy
    height, width = integral_tiles.shape[1], integral_tiles.shape[2]
    filled, local_index, slot_position = bucket_slots(
        tile_reader, tile_k, tile_column, targets, SLOT
    )
    picked = jnp.take(integral_tiles, local_index.reshape(-1), axis=0)
    picked = jnp.where(filled.reshape(-1)[:, None, None] > 0, picked, 0.0)
    label = jnp.zeros((targets, 1, width), jnp.float32).at[:, 0, :SLOT].set(
        slot_position.reshape(targets, SLOT).astype(jnp.float32)
    )
    outgoing = jnp.concatenate([picked.reshape(targets, SLOT * height, width), label], axis=1)
    arrived = bulk_exchange(outgoing, targets, nxy)
    position = arrived[:, SLOT * height, :SLOT].reshape(-1).astype(jnp.int32)
    arrived = arrived[:, : SLOT * height, :].reshape(targets * SLOT, height * width)
    table = (position[None, :] == jnp.arange(KT * CT, dtype=jnp.int32)[:, None]).astype(jnp.float32)
    placed = jnp.dot(table, arrived, precision=lax.Precision.HIGHEST)
    placed = placed.reshape(KT, CT, height, width).transpose(0, 2, 1, 3).reshape(KT * height, CT * width)
    nz = lax.axis_size("zl")
    gathered = row_gather(placed, nz)
    dense = gathered.reshape(-1, CT * width)
    pair = lax.all_gather(amplitudes, "zh", axis=0, tiled=False)
    blocks = lax.all_gather(pair, "xy", axis=0, tiled=False)
    rows, own_cols = amplitudes.shape
    amps = blocks.transpose(2, 1, 0, 3).reshape(rows, targets * own_cols)
    groups = gathered.shape[0]
    amps = amps.reshape(rows, KT, groups, height).transpose(0, 2, 1, 3).reshape(rows, -1)
    return residual_in + jnp.dot(amps, dense, precision=lax.Precision.HIGH)


def solution(mesh):
    row_size = mesh.shape["row"]
    bulk_size = mesh.shape["bulk"]
    devices = np.asarray(mesh.devices).reshape(row_size // 2, 2, Z_HALVES, bulk_size // Z_HALVES)
    inner = Mesh(devices, ("zl", "core", "zh", "xy"))
    row = ("zl", "core")
    bulk = ("zh", "xy")
    placed = (
        P(row, bulk),
        P(row, bulk),
        P(bulk, row, None),
        P(bulk, None),
        P(bulk),
        P(bulk),
    )
    return jax.shard_map(
        local, mesh=inner, in_specs=placed, out_specs=P(row, bulk), check_vma=False
    )
```

```python
import functools

import jax
import jax.numpy as jnp
import numpy as np
from jax import lax
from jax.experimental import pallas as pl
from jax.experimental.pallas import tpu as pltpu
from jax.sharding import Mesh, PartitionSpec as P

MESH = pl.DeviceIdType.MESH

KT = 16
CT = 8
SLOT = 2
Z_HALVES = 2


def bucket_slots(tile_reader, tile_k, tile_column, targets, slots):
    readers = tile_reader[:, 0]
    matches = (readers[:, None] == jnp.arange(targets, dtype=jnp.int32)[None, :]).astype(jnp.int32)
    ordinal = jnp.cumsum(matches, axis=0) - matches
    position = jnp.sum(ordinal * matches, axis=1)
    select = matches.T[:, None, :] * (
        position[None, None, :] == jnp.arange(slots, dtype=jnp.int32)[None, :, None]
    ).astype(jnp.int32)
    filled = jnp.sum(select, axis=2)
    local_index = jnp.sum(select * jnp.arange(readers.shape[0], dtype=jnp.int32)[None, None, :], axis=2)
    slot_position = jnp.sum(select * (tile_k * CT + tile_column)[None, None, :], axis=2) + filled - 1
    return filled, local_index, slot_position


def gather_kernel(nz, src_ref, out_ref, local_sem, send_sem, recv_sem):
    zl = lax.axis_index("zl")
    c = lax.axis_index("core")
    zh = lax.axis_index("zh")
    xy = lax.axis_index("xy")
    partner = (zl, 1 - c, zh, xy)
    left = (zl - 1, c, zh, xy)
    right = (zl + 1, c, zh, xy)
    has_left = zl > 0
    has_right = zl < nz - 1
    own = zl * 2 + c

    barrier = pltpu.get_barrier_semaphore()
    pl.semaphore_signal(barrier, 1, device_id=partner, device_id_type=MESH)

    @pl.when(has_left)
    def _():
        pl.semaphore_signal(barrier, 1, device_id=left, device_id_type=MESH)

    @pl.when(has_right)
    def _():
        pl.semaphore_signal(barrier, 1, device_id=right, device_id_type=MESH)

    peers = 1 + has_left.astype(jnp.int32) + has_right.astype(jnp.int32)
    pl.semaphore_wait(barrier, peers)

    def copy(src, slot, kind, dev):
        return pltpu.make_async_remote_copy(
            src_ref=src,
            dst_ref=out_ref.at[slot],
            send_sem=send_sem.at[slot, kind],
            recv_sem=recv_sem.at[slot],
            device_id=dev,
            device_id_type=MESH,
        )

    mine = pltpu.make_async_copy(src_ref, out_ref.at[own], local_sem)
    mine.start()
    copy(src_ref, own, 0, partner).start()

    @pl.when(has_left)
    def _():
        copy(src_ref, own, 1, left).start()

    @pl.when(has_right)
    def _():
        copy(src_ref, own, 2, right).start()

    for d in range(1, nz):
        @pl.when(zl - d >= 0)
        def _():
            s = (zl - d) * 2 + c
            copy(out_ref.at[s], s, 0, partner).wait_recv()
            copy(out_ref.at[s], s, 0, partner).start()

            @pl.when(has_right)
            def _():
                copy(out_ref.at[s], s, 2, right).start()

        @pl.when(zl + d <= nz - 1)
        def _():
            s = (zl + d) * 2 + c
            copy(out_ref.at[s], s, 0, partner).wait_recv()
            copy(out_ref.at[s], s, 0, partner).start()

            @pl.when(has_left)
            def _():
                copy(out_ref.at[s], s, 1, left).start()

    for z in range(nz):
        s = z * 2 + (1 - c)
        copy(out_ref.at[s], s, 0, partner).wait_recv()

    mine.wait()
    for z in range(nz):
        s = z * 2 + c
        copy(out_ref.at[s], s, 0, partner).wait_send()

        @pl.when(has_left & (z >= zl))
        def _():
            copy(out_ref.at[s], s, 1, left).wait_send()

        @pl.when(has_right & (z <= zl))
        def _():
            copy(out_ref.at[s], s, 2, right).wait_send()


def row_gather(placed, nz):
    groups = 2 * nz
    return pl.pallas_call(
        functools.partial(gather_kernel, nz),
        out_shape=jax.ShapeDtypeStruct((groups,) + placed.shape, placed.dtype),
        in_specs=[pl.BlockSpec(memory_space=pltpu.VMEM)],
        out_specs=pl.BlockSpec(memory_space=pltpu.VMEM),
        scratch_shapes=[
            pltpu.SemaphoreType.DMA(()),
            pltpu.SemaphoreType.DMA((groups, 3)),
            pltpu.SemaphoreType.DMA((groups,)),
        ],
        compiler_params=pltpu.CompilerParams(collective_id=0, has_side_effects=True),
    )(placed)


def exchange_kernel(nb, nxy, src_ref, out_ref, local_sem, send_sem, recv_sem):
    zl = lax.axis_index("zl")
    c = lax.axis_index("core")
    me = lax.axis_index("zh") * nxy + lax.axis_index("xy")

    def peer(b):
        return (zl, c, b // nxy, lax.rem(b, nxy))

    barrier = pltpu.get_barrier_semaphore()

    def greet(p, carry):
        pl.semaphore_signal(barrier, 1, device_id=peer(lax.rem(me + p, nb)), device_id_type=MESH)
        return carry

    lax.fori_loop(1, nb, greet, 0)
    pl.semaphore_wait(barrier, nb - 1)

    mine = pltpu.make_async_copy(src_ref.at[me], out_ref.at[me], local_sem)
    mine.start()

    def copy(p, dest):
        return pltpu.make_async_remote_copy(
            src_ref=src_ref.at[dest],
            dst_ref=out_ref.at[me],
            send_sem=send_sem.at[p],
            recv_sem=recv_sem.at[me],
            device_id=peer(dest),
            device_id_type=MESH,
        )

    def send(p, carry):
        copy(p, lax.rem(me + p, nb)).start()
        return carry

    lax.fori_loop(1, nb, send, 0)

    def receive(p, carry):
        source = lax.rem(me + nb - p, nb)
        pltpu.make_async_remote_copy(
            src_ref=src_ref.at[source],
            dst_ref=out_ref.at[source],
            send_sem=send_sem.at[p],
            recv_sem=recv_sem.at[source],
            device_id=peer(source),
            device_id_type=MESH,
        ).wait_recv()
        return carry

    lax.fori_loop(1, nb, receive, 0)
    mine.wait()

    def sent(p, carry):
        copy(p, lax.rem(me + p, nb)).wait_send()
        return carry

    lax.fori_loop(1, nb, sent, 0)


def bulk_exchange(outgoing, nb, nxy):
    return pl.pallas_call(
        functools.partial(exchange_kernel, nb, nxy),
        out_shape=jax.ShapeDtypeStruct(outgoing.shape, outgoing.dtype),
        in_specs=[pl.BlockSpec(memory_space=pltpu.VMEM)],
        out_specs=pl.BlockSpec(memory_space=pltpu.VMEM),
        scratch_shapes=[
            pltpu.SemaphoreType.DMA(()),
            pltpu.SemaphoreType.DMA((nb,)),
            pltpu.SemaphoreType.DMA((nb,)),
        ],
        compiler_params=pltpu.CompilerParams(collective_id=1, has_side_effects=True),
    )(outgoing)


def local(residual_in, amplitudes, integral_tiles, tile_reader, tile_k, tile_column):
    nxy = lax.axis_size("xy")
    targets = lax.axis_size("zh") * nxy
    height, width = integral_tiles.shape[1], integral_tiles.shape[2]
    filled, local_index, slot_position = bucket_slots(
        tile_reader, tile_k, tile_column, targets, SLOT
    )
    picked = jnp.take(integral_tiles, local_index.reshape(-1), axis=0)
    picked = jnp.where(filled.reshape(-1)[:, None, None] > 0, picked, 0.0)
    label = jnp.zeros((targets, 1, width), jnp.float32).at[:, 0, :SLOT].set(
        slot_position.reshape(targets, SLOT).astype(jnp.float32)
    )
    outgoing = jnp.concatenate([picked.reshape(targets, SLOT * height, width), label], axis=1)
    arrived = bulk_exchange(outgoing, targets, nxy)
    position = arrived[:, SLOT * height, :SLOT].reshape(-1).astype(jnp.int32)
    arrived = arrived[:, : SLOT * height, :].reshape(targets * SLOT, height * width)
    table = (position[None, :] == jnp.arange(KT * CT, dtype=jnp.int32)[:, None]).astype(jnp.float32)
    placed = jnp.dot(table, arrived, precision=lax.Precision.HIGHEST)
    placed = placed.reshape(KT, CT, height, width).transpose(0, 2, 1, 3).reshape(KT * height, CT * width)
    nz = lax.axis_size("zl")
    gathered = row_gather(placed, nz)
    dense = gathered.reshape(-1, CT * width)
    halves = lax.axis_size("zh")
    other = lax.ppermute(amplitudes, "zh", perm=[(h, (h + 1) % halves) for h in range(halves)])
    pair = jnp.stack([amplitudes, other])
    blocks = lax.all_gather(pair, "xy", axis=0, tiled=False)
    blocks = jnp.where(lax.axis_index("zh") == 0, blocks, blocks[:, ::-1])
    rows, own_cols = amplitudes.shape
    amps = blocks.transpose(2, 1, 0, 3).reshape(rows, targets * own_cols)
    groups = gathered.shape[0]
    amps = amps.reshape(rows, KT, groups, height).transpose(0, 2, 1, 3).reshape(rows, -1)
    return residual_in + jnp.dot(amps, dense, precision=lax.Precision.HIGH)


def solution(mesh):
    row_size = mesh.shape["row"]
    bulk_size = mesh.shape["bulk"]
    devices = np.asarray(mesh.devices).reshape(row_size // 2, 2, Z_HALVES, bulk_size // Z_HALVES)
    inner = Mesh(devices, ("zl", "core", "zh", "xy"))
    row = ("zl", "core")
    bulk = ("zh", "xy")
    placed = (
        P(row, bulk),
        P(row, bulk),
        P(bulk, row, None),
        P(bulk, None),
        P(bulk),
        P(bulk),
    )
    return jax.shard_map(
        local, mesh=inner, in_specs=placed, out_specs=P(row, bulk), check_vma=False
    )
```

```python
import functools

import jax
import jax.numpy as jnp
import numpy as np
from jax import lax
from jax.experimental import pallas as pl
from jax.experimental.pallas import tpu as pltpu
from jax.sharding import Mesh, PartitionSpec as P

MESH = pl.DeviceIdType.MESH

KT = 16
CT = 8
SLOT = 2
Z_HALVES = 2


def bucket_slots(tile_reader, tile_k, tile_column, targets, slots):
    readers = tile_reader[:, 0]
    matches = (readers[:, None] == jnp.arange(targets, dtype=jnp.int32)[None, :]).astype(jnp.int32)
    ordinal = jnp.cumsum(matches, axis=0) - matches
    position = jnp.sum(ordinal * matches, axis=1)
    select = matches.T[:, None, :] * (
        position[None, None, :] == jnp.arange(slots, dtype=jnp.int32)[None, :, None]
    ).astype(jnp.int32)
    filled = jnp.sum(select, axis=2)
    local_index = jnp.sum(select * jnp.arange(readers.shape[0], dtype=jnp.int32)[None, None, :], axis=2)
    slot_position = jnp.sum(select * (tile_k * CT + tile_column)[None, None, :], axis=2) + filled - 1
    return filled, local_index, slot_position


def gather_kernel(nz, src_ref, out_ref, local_sem, send_sem, recv_sem):
    zl = lax.axis_index("zl")
    c = lax.axis_index("core")
    zh = lax.axis_index("zh")
    xy = lax.axis_index("xy")
    partner = (zl, 1 - c, zh, xy)
    left = (zl - 1, c, zh, xy)
    right = (zl + 1, c, zh, xy)
    has_left = zl > 0
    has_right = zl < nz - 1
    own = zl * 2 + c

    barrier = pltpu.get_barrier_semaphore()
    pl.semaphore_signal(barrier, 1, device_id=partner, device_id_type=MESH)

    @pl.when(has_left)
    def _():
        pl.semaphore_signal(barrier, 1, device_id=left, device_id_type=MESH)

    @pl.when(has_right)
    def _():
        pl.semaphore_signal(barrier, 1, device_id=right, device_id_type=MESH)

    peers = 1 + has_left.astype(jnp.int32) + has_right.astype(jnp.int32)
    pl.semaphore_wait(barrier, peers)

    def copy(src, slot, kind, dev):
        return pltpu.make_async_remote_copy(
            src_ref=src,
            dst_ref=out_ref.at[slot],
            send_sem=send_sem.at[slot, kind],
            recv_sem=recv_sem.at[slot],
            device_id=dev,
            device_id_type=MESH,
        )

    mine = pltpu.make_async_copy(src_ref, out_ref.at[own], local_sem)
    mine.start()
    copy(src_ref, own, 0, partner).start()

    @pl.when(has_left)
    def _():
        copy(src_ref, own, 1, left).start()

    @pl.when(has_right)
    def _():
        copy(src_ref, own, 2, right).start()

    for d in range(1, nz):
        @pl.when(zl - d >= 0)
        def _():
            s = (zl - d) * 2 + c
            copy(out_ref.at[s], s, 0, partner).wait_recv()
            copy(out_ref.at[s], s, 0, partner).start()

            @pl.when(has_right)
            def _():
                copy(out_ref.at[s], s, 2, right).start()

        @pl.when(zl + d <= nz - 1)
        def _():
            s = (zl + d) * 2 + c
            copy(out_ref.at[s], s, 0, partner).wait_recv()
            copy(out_ref.at[s], s, 0, partner).start()

            @pl.when(has_left)
            def _():
                copy(out_ref.at[s], s, 1, left).start()

    for z in range(nz):
        s = z * 2 + (1 - c)
        copy(out_ref.at[s], s, 0, partner).wait_recv()

    mine.wait()
    for z in range(nz):
        s = z * 2 + c
        copy(out_ref.at[s], s, 0, partner).wait_send()

        @pl.when(has_left & (z >= zl))
        def _():
            copy(out_ref.at[s], s, 1, left).wait_send()

        @pl.when(has_right & (z <= zl))
        def _():
            copy(out_ref.at[s], s, 2, right).wait_send()


def row_gather(placed, nz):
    groups = 2 * nz
    return pl.pallas_call(
        functools.partial(gather_kernel, nz),
        out_shape=jax.ShapeDtypeStruct((groups,) + placed.shape, placed.dtype),
        in_specs=[pl.BlockSpec(memory_space=pltpu.VMEM)],
        out_specs=pl.BlockSpec(memory_space=pltpu.VMEM),
        scratch_shapes=[
            pltpu.SemaphoreType.DMA(()),
            pltpu.SemaphoreType.DMA((groups, 3)),
            pltpu.SemaphoreType.DMA((groups,)),
        ],
        compiler_params=pltpu.CompilerParams(collective_id=0, has_side_effects=True),
    )(placed)


def exchange_kernel(nb, nxy, src_ref, mine_ref, out_ref, other_ref, local_sem, send_sem, recv_sem,
                    pair_sem):
    zl = lax.axis_index("zl")
    c = lax.axis_index("core")
    me = lax.axis_index("zh") * nxy + lax.axis_index("xy")

    def peer(b):
        return (zl, c, b // nxy, lax.rem(b, nxy))

    barrier = pltpu.get_barrier_semaphore()

    def greet(p, carry):
        pl.semaphore_signal(barrier, 1, device_id=peer(lax.rem(me + p, nb)), device_id_type=MESH)
        return carry

    lax.fori_loop(1, nb, greet, 0)
    pl.semaphore_wait(barrier, nb - 1)

    mine = pltpu.make_async_copy(src_ref.at[me], out_ref.at[me], local_sem)
    mine.start()

    def copy(p, dest):
        return pltpu.make_async_remote_copy(
            src_ref=src_ref.at[dest],
            dst_ref=out_ref.at[me],
            send_sem=send_sem.at[p],
            recv_sem=recv_sem.at[me],
            device_id=peer(dest),
            device_id_type=MESH,
        )

    def send(p, carry):
        copy(p, lax.rem(me + p, nb)).start()
        return carry

    lax.fori_loop(1, nb, send, 0)

    twin = lax.rem(me + nb // 2, nb)
    pair_copy = pltpu.make_async_remote_copy(
        src_ref=mine_ref,
        dst_ref=other_ref,
        send_sem=pair_sem.at[0],
        recv_sem=pair_sem.at[1],
        device_id=peer(twin),
        device_id_type=MESH,
    )
    pair_copy.start()

    def receive(p, carry):
        source = lax.rem(me + nb - p, nb)
        pltpu.make_async_remote_copy(
            src_ref=src_ref.at[source],
            dst_ref=out_ref.at[source],
            send_sem=send_sem.at[p],
            recv_sem=recv_sem.at[source],
            device_id=peer(source),
            device_id_type=MESH,
        ).wait_recv()
        return carry

    lax.fori_loop(1, nb, receive, 0)
    mine.wait()
    pair_copy.wait_recv()
    pair_copy.wait_send()

    def sent(p, carry):
        copy(p, lax.rem(me + p, nb)).wait_send()
        return carry

    lax.fori_loop(1, nb, sent, 0)


def bulk_exchange(outgoing, mine_t, nb, nxy):
    return pl.pallas_call(
        functools.partial(exchange_kernel, nb, nxy),
        out_shape=(
            jax.ShapeDtypeStruct(outgoing.shape, outgoing.dtype),
            jax.ShapeDtypeStruct(mine_t.shape, mine_t.dtype),
        ),
        in_specs=[pl.BlockSpec(memory_space=pltpu.VMEM)] * 2,
        out_specs=(pl.BlockSpec(memory_space=pltpu.VMEM), pl.BlockSpec(memory_space=pltpu.VMEM)),
        scratch_shapes=[
            pltpu.SemaphoreType.DMA(()),
            pltpu.SemaphoreType.DMA((nb,)),
            pltpu.SemaphoreType.DMA((nb,)),
            pltpu.SemaphoreType.DMA((2,)),
        ],
        compiler_params=pltpu.CompilerParams(collective_id=1, has_side_effects=True),
    )(outgoing, mine_t)


def local(residual_in, amplitudes, integral_tiles, tile_reader, tile_k, tile_column):
    nxy = lax.axis_size("xy")
    targets = lax.axis_size("zh") * nxy
    height, width = integral_tiles.shape[1], integral_tiles.shape[2]
    filled, local_index, slot_position = bucket_slots(
        tile_reader, tile_k, tile_column, targets, SLOT
    )
    picked = jnp.take(integral_tiles, local_index.reshape(-1), axis=0)
    picked = jnp.where(filled.reshape(-1)[:, None, None] > 0, picked, 0.0)
    label = jnp.zeros((targets, 1, width), jnp.float32).at[:, 0, :SLOT].set(
        slot_position.reshape(targets, SLOT).astype(jnp.float32)
    )
    outgoing = jnp.concatenate([picked.reshape(targets, SLOT * height, width), label], axis=1)
    arrived, other_t = bulk_exchange(outgoing, amplitudes.T, targets, nxy)
    position = arrived[:, SLOT * height, :SLOT].reshape(-1).astype(jnp.int32)
    arrived = arrived[:, : SLOT * height, :].reshape(targets * SLOT, height * width)
    table = (position[None, :] == jnp.arange(KT * CT, dtype=jnp.int32)[:, None]).astype(jnp.float32)
    placed = jnp.dot(table, arrived, precision=lax.Precision.HIGHEST)
    placed = placed.reshape(KT, CT, height, width).transpose(0, 2, 1, 3).reshape(KT * height, CT * width)
    nz = lax.axis_size("zl")
    gathered = row_gather(placed, nz)
    dense = gathered.reshape(-1, CT * width)
    pair = jnp.stack([amplitudes, other_t.T])
    blocks = lax.all_gather(pair, "xy", axis=0, tiled=False)
    blocks = jnp.where(lax.axis_index("zh") == 0, blocks, blocks[:, ::-1])
    rows, own_cols = amplitudes.shape
    amps = blocks.transpose(2, 1, 0, 3).reshape(rows, targets * own_cols)
    groups = gathered.shape[0]
    amps = amps.reshape(rows, KT, groups, height).transpose(0, 2, 1, 3).reshape(rows, -1)
    return residual_in + jnp.dot(amps, dense, precision=lax.Precision.HIGH)


def solution(mesh):
    row_size = mesh.shape["row"]
    bulk_size = mesh.shape["bulk"]
    devices = np.asarray(mesh.devices).reshape(row_size // 2, 2, Z_HALVES, bulk_size // Z_HALVES)
    inner = Mesh(devices, ("zl", "core", "zh", "xy"))
    row = ("zl", "core")
    bulk = ("zh", "xy")
    placed = (
        P(row, bulk),
        P(row, bulk),
        P(bulk, row, None),
        P(bulk, None),
        P(bulk),
        P(bulk),
    )
    return jax.shard_map(
        local, mesh=inner, in_specs=placed, out_specs=P(row, bulk), check_vma=False
    )
```

```python
import functools

import jax
import jax.numpy as jnp
import numpy as np
from jax import lax
from jax.experimental import pallas as pl
from jax.experimental.pallas import tpu as pltpu
from jax.sharding import Mesh, PartitionSpec as P

MESH = pl.DeviceIdType.MESH

KT = 16
CT = 8
SLOT = 2
Z_HALVES = 2


def bucket_slots(tile_reader, tile_k, tile_column, targets, slots):
    readers = tile_reader[:, 0]
    matches = (readers[:, None] == jnp.arange(targets, dtype=jnp.int32)[None, :]).astype(jnp.int32)
    ordinal = jnp.cumsum(matches, axis=0) - matches
    position = jnp.sum(ordinal * matches, axis=1)
    select = matches.T[:, None, :] * (
        position[None, None, :] == jnp.arange(slots, dtype=jnp.int32)[None, :, None]
    ).astype(jnp.int32)
    filled = jnp.sum(select, axis=2)
    local_index = jnp.sum(select * jnp.arange(readers.shape[0], dtype=jnp.int32)[None, None, :], axis=2)
    slot_position = jnp.sum(select * (tile_k * CT + tile_column)[None, None, :], axis=2) + filled - 1
    return filled, local_index, slot_position


def gather_kernel(nz, src_ref, out_ref, local_sem, send_sem, recv_sem):
    zl = lax.axis_index("zl")
    c = lax.axis_index("core")
    zh = lax.axis_index("zh")
    xy = lax.axis_index("xy")
    partner = (zl, 1 - c, zh, xy)
    left = (zl - 1, c, zh, xy)
    right = (zl + 1, c, zh, xy)
    has_left = zl > 0
    has_right = zl < nz - 1
    own = zl * 2 + c

    barrier = pltpu.get_barrier_semaphore()
    pl.semaphore_signal(barrier, 1, device_id=partner, device_id_type=MESH)

    @pl.when(has_left)
    def _():
        pl.semaphore_signal(barrier, 1, device_id=left, device_id_type=MESH)

    @pl.when(has_right)
    def _():
        pl.semaphore_signal(barrier, 1, device_id=right, device_id_type=MESH)

    peers = 1 + has_left.astype(jnp.int32) + has_right.astype(jnp.int32)
    pl.semaphore_wait(barrier, peers)

    def copy(src, slot, kind, dev):
        return pltpu.make_async_remote_copy(
            src_ref=src,
            dst_ref=out_ref.at[slot],
            send_sem=send_sem.at[slot, kind],
            recv_sem=recv_sem.at[slot],
            device_id=dev,
            device_id_type=MESH,
        )

    mine = pltpu.make_async_copy(src_ref, out_ref.at[own], local_sem)
    mine.start()
    copy(src_ref, own, 0, partner).start()

    @pl.when(has_left)
    def _():
        copy(src_ref, own, 1, left).start()

    @pl.when(has_right)
    def _():
        copy(src_ref, own, 2, right).start()

    for d in range(1, nz):
        @pl.when(zl - d >= 0)
        def _():
            s = (zl - d) * 2 + c
            copy(out_ref.at[s], s, 0, partner).wait_recv()
            copy(out_ref.at[s], s, 0, partner).start()

            @pl.when(has_right)
            def _():
                copy(out_ref.at[s], s, 2, right).start()

        @pl.when(zl + d <= nz - 1)
        def _():
            s = (zl + d) * 2 + c
            copy(out_ref.at[s], s, 0, partner).wait_recv()
            copy(out_ref.at[s], s, 0, partner).start()

            @pl.when(has_left)
            def _():
                copy(out_ref.at[s], s, 1, left).start()

    for z in range(nz):
        s = z * 2 + (1 - c)
        copy(out_ref.at[s], s, 0, partner).wait_recv()

    mine.wait()
    for z in range(nz):
        s = z * 2 + c
        copy(out_ref.at[s], s, 0, partner).wait_send()

        @pl.when(has_left & (z >= zl))
        def _():
            copy(out_ref.at[s], s, 1, left).wait_send()

        @pl.when(has_right & (z <= zl))
        def _():
            copy(out_ref.at[s], s, 2, right).wait_send()


def row_gather(placed, nz):
    groups = 2 * nz
    return pl.pallas_call(
        functools.partial(gather_kernel, nz),
        out_shape=jax.ShapeDtypeStruct((groups,) + placed.shape, placed.dtype),
        in_specs=[pl.BlockSpec(memory_space=pltpu.VMEM)],
        out_specs=pl.BlockSpec(memory_space=pltpu.VMEM),
        scratch_shapes=[
            pltpu.SemaphoreType.DMA(()),
            pltpu.SemaphoreType.DMA((groups, 3)),
            pltpu.SemaphoreType.DMA((groups,)),
        ],
        compiler_params=pltpu.CompilerParams(collective_id=0, has_side_effects=True),
    )(placed)


def exchange_kernel(nb, nxy, src_ref, mine_ref, out_ref, other_ref, local_sem, send_sem, recv_sem,
                    pair_sem):
    zl = lax.axis_index("zl")
    c = lax.axis_index("core")
    me = lax.axis_index("zh") * nxy + lax.axis_index("xy")

    def peer(b):
        return (zl, c, b // nxy, lax.rem(b, nxy))

    barrier = pltpu.get_barrier_semaphore()

    def greet(p, carry):
        pl.semaphore_signal(barrier, 1, device_id=peer(lax.rem(me + p, nb)), device_id_type=MESH)
        return carry

    lax.fori_loop(1, nb, greet, 0)
    pl.semaphore_wait(barrier, nb - 1)

    mine = pltpu.make_async_copy(src_ref.at[me], out_ref.at[me], local_sem)
    mine.start()

    def copy(p, dest):
        return pltpu.make_async_remote_copy(
            src_ref=src_ref.at[dest],
            dst_ref=out_ref.at[me],
            send_sem=send_sem.at[p],
            recv_sem=recv_sem.at[me],
            device_id=peer(dest),
            device_id_type=MESH,
        )

    def send(p, carry):
        copy(p, lax.rem(me + p, nb)).start()
        return carry

    lax.fori_loop(1, nb, send, 0)

    twin = lax.rem(me + nb // 2, nb)
    pair_copy = pltpu.make_async_remote_copy(
        src_ref=mine_ref,
        dst_ref=other_ref,
        send_sem=pair_sem.at[0],
        recv_sem=pair_sem.at[1],
        device_id=peer(twin),
        device_id_type=MESH,
    )
    pair_copy.start()

    def receive(p, carry):
        source = lax.rem(me + nb - p, nb)
        pltpu.make_async_remote_copy(
            src_ref=src_ref.at[source],
            dst_ref=out_ref.at[source],
            send_sem=send_sem.at[p],
            recv_sem=recv_sem.at[source],
            device_id=peer(source),
            device_id_type=MESH,
        ).wait_recv()
        return carry

    lax.fori_loop(1, nb, receive, 0)
    mine.wait()
    pair_copy.wait_recv()
    pair_copy.wait_send()

    def sent(p, carry):
        copy(p, lax.rem(me + p, nb)).wait_send()
        return carry

    lax.fori_loop(1, nb, sent, 0)


def bulk_exchange(outgoing, mine_t, nb, nxy):
    return pl.pallas_call(
        functools.partial(exchange_kernel, nb, nxy),
        out_shape=(
            jax.ShapeDtypeStruct(outgoing.shape, outgoing.dtype),
            jax.ShapeDtypeStruct(mine_t.shape, mine_t.dtype),
        ),
        in_specs=[pl.BlockSpec(memory_space=pltpu.VMEM)] * 2,
        out_specs=(pl.BlockSpec(memory_space=pltpu.VMEM), pl.BlockSpec(memory_space=pltpu.VMEM)),
        scratch_shapes=[
            pltpu.SemaphoreType.DMA(()),
            pltpu.SemaphoreType.DMA((nb,)),
            pltpu.SemaphoreType.DMA((nb,)),
            pltpu.SemaphoreType.DMA((2,)),
        ],
        compiler_params=pltpu.CompilerParams(collective_id=1, has_side_effects=True),
    )(outgoing, mine_t)


def local(residual_in, amplitudes, integral_tiles, tile_reader, tile_k, tile_column):
    nxy = lax.axis_size("xy")
    targets = lax.axis_size("zh") * nxy
    height, width = integral_tiles.shape[1], integral_tiles.shape[2]
    filled, local_index, slot_position = bucket_slots(
        tile_reader, tile_k, tile_column, targets, SLOT
    )
    picked = jnp.take(integral_tiles, local_index.reshape(-1), axis=0)
    picked = jnp.where(filled.reshape(-1)[:, None, None] > 0, picked, 0.0)
    label = jnp.zeros((targets, 1, width), jnp.float32).at[:, 0, :SLOT].set(
        slot_position.reshape(targets, SLOT).astype(jnp.float32)
    )
    outgoing = jnp.concatenate([picked.reshape(targets, SLOT * height, width), label], axis=1)
    arrived, other_t = bulk_exchange(outgoing, amplitudes.T, targets, nxy)
    position = arrived[:, SLOT * height, :SLOT].reshape(-1).astype(jnp.int32)
    arrived = arrived[:, : SLOT * height, :].reshape(targets * SLOT, height * width)
    table = (position[None, :] == jnp.arange(KT * CT, dtype=jnp.int32)[:, None]).astype(jnp.float32)
    placed = jnp.dot(table, arrived, precision=lax.Precision.HIGHEST)
    placed = placed.reshape(KT, CT, height, width).transpose(0, 2, 1, 3).reshape(KT * height, CT * width)
    nz = lax.axis_size("zl")
    gathered = row_gather(placed, nz)
    dense = gathered.reshape(-1, CT * width)
    other = other_t.T
    lower = lax.axis_index("zh") == 0
    pair = jnp.stack([jnp.where(lower, amplitudes, other), jnp.where(lower, other, amplitudes)])
    blocks = lax.all_gather(pair, "xy", axis=0, tiled=False)
    rows, own_cols = amplitudes.shape
    amps = blocks.transpose(2, 1, 0, 3).reshape(rows, targets * own_cols)
    groups = gathered.shape[0]
    amps = amps.reshape(rows, KT, groups, height).transpose(0, 2, 1, 3).reshape(rows, -1)
    return residual_in + jnp.dot(amps, dense, precision=lax.Precision.HIGH)


def solution(mesh):
    row_size = mesh.shape["row"]
    bulk_size = mesh.shape["bulk"]
    devices = np.asarray(mesh.devices).reshape(row_size // 2, 2, Z_HALVES, bulk_size // Z_HALVES)
    inner = Mesh(devices, ("zl", "core", "zh", "xy"))
    row = ("zl", "core")
    bulk = ("zh", "xy")
    placed = (
        P(row, bulk),
        P(row, bulk),
        P(bulk, row, None),
        P(bulk, None),
        P(bulk),
        P(bulk),
    )
    return jax.shard_map(
        local, mesh=inner, in_specs=placed, out_specs=P(row, bulk), check_vma=False
    )
```

```python
import functools

import jax
import jax.numpy as jnp
import numpy as np
from jax import lax
from jax.experimental import pallas as pl
from jax.experimental.pallas import tpu as pltpu
from jax.sharding import Mesh, PartitionSpec as P

MESH = pl.DeviceIdType.MESH

KT = 16
CT = 8
SLOT = 2
Z_HALVES = 2
RELAY_PARTS = 2


def bucket_slots(tile_reader, tile_k, tile_column, targets, slots):
    readers = tile_reader[:, 0]
    matches = (readers[:, None] == jnp.arange(targets, dtype=jnp.int32)[None, :]).astype(jnp.int32)
    ordinal = jnp.cumsum(matches, axis=0) - matches
    position = jnp.sum(ordinal * matches, axis=1)
    select = matches.T[:, None, :] * (
        position[None, None, :] == jnp.arange(slots, dtype=jnp.int32)[None, :, None]
    ).astype(jnp.int32)
    filled = jnp.sum(select, axis=2)
    local_index = jnp.sum(select * jnp.arange(readers.shape[0], dtype=jnp.int32)[None, None, :], axis=2)
    slot_position = jnp.sum(select * (tile_k * CT + tile_column)[None, None, :], axis=2) + filled - 1
    return filled, local_index, slot_position


def gather_kernel(nz, parts, src_ref, out_ref, local_sem, send_sem, recv_sem):
    zl = lax.axis_index("zl")
    c = lax.axis_index("core")
    zh = lax.axis_index("zh")
    xy = lax.axis_index("xy")
    partner = (zl, 1 - c, zh, xy)
    left = (zl - 1, c, zh, xy)
    right = (zl + 1, c, zh, xy)
    has_left = zl > 0
    has_right = zl < nz - 1
    own = zl * 2 + c

    barrier = pltpu.get_barrier_semaphore()
    pl.semaphore_signal(barrier, 1, device_id=partner, device_id_type=MESH)

    @pl.when(has_left)
    def _():
        pl.semaphore_signal(barrier, 1, device_id=left, device_id_type=MESH)

    @pl.when(has_right)
    def _():
        pl.semaphore_signal(barrier, 1, device_id=right, device_id_type=MESH)

    peers = 1 + has_left.astype(jnp.int32) + has_right.astype(jnp.int32)
    pl.semaphore_wait(barrier, peers)

    piece = src_ref.shape[0] // parts

    def copy(src, slot, kind, dev, q):
        rows = pl.ds(q * piece, piece)
        return pltpu.make_async_remote_copy(
            src_ref=src.at[rows],
            dst_ref=out_ref.at[slot, rows],
            send_sem=send_sem.at[slot, q, kind],
            recv_sem=recv_sem.at[slot, q],
            device_id=dev,
            device_id_type=MESH,
        )

    mine = pltpu.make_async_copy(src_ref, out_ref.at[own], local_sem)
    mine.start()
    for q in range(parts):
        copy(src_ref, own, 0, partner, q).start()

        @pl.when(has_left)
        def _():
            copy(src_ref, own, 1, left, q).start()

        @pl.when(has_right)
        def _():
            copy(src_ref, own, 2, right, q).start()

    for d in range(1, nz):
        for q in range(parts):
            @pl.when(zl - d >= 0)
            def _():
                s = (zl - d) * 2 + c
                copy(out_ref.at[s], s, 0, partner, q).wait_recv()
                copy(out_ref.at[s], s, 0, partner, q).start()

                @pl.when(has_right)
                def _():
                    copy(out_ref.at[s], s, 2, right, q).start()

            @pl.when(zl + d <= nz - 1)
            def _():
                s = (zl + d) * 2 + c
                copy(out_ref.at[s], s, 0, partner, q).wait_recv()
                copy(out_ref.at[s], s, 0, partner, q).start()

                @pl.when(has_left)
                def _():
                    copy(out_ref.at[s], s, 1, left, q).start()

    for z in range(nz):
        s = z * 2 + (1 - c)
        for q in range(parts):
            copy(out_ref.at[s], s, 0, partner, q).wait_recv()

    mine.wait()
    for z in range(nz):
        s = z * 2 + c
        for q in range(parts):
            copy(out_ref.at[s], s, 0, partner, q).wait_send()

            @pl.when(has_left & (z >= zl))
            def _():
                copy(out_ref.at[s], s, 1, left, q).wait_send()

            @pl.when(has_right & (z <= zl))
            def _():
                copy(out_ref.at[s], s, 2, right, q).wait_send()


def row_gather(placed, nz):
    groups = 2 * nz
    return pl.pallas_call(
        functools.partial(gather_kernel, nz, RELAY_PARTS),
        out_shape=jax.ShapeDtypeStruct((groups,) + placed.shape, placed.dtype),
        in_specs=[pl.BlockSpec(memory_space=pltpu.VMEM)],
        out_specs=pl.BlockSpec(memory_space=pltpu.VMEM),
        scratch_shapes=[
            pltpu.SemaphoreType.DMA(()),
            pltpu.SemaphoreType.DMA((groups, RELAY_PARTS, 3)),
            pltpu.SemaphoreType.DMA((groups, RELAY_PARTS)),
        ],
        compiler_params=pltpu.CompilerParams(collective_id=0, has_side_effects=True),
    )(placed)


def exchange_kernel(nb, nxy, src_ref, mine_ref, out_ref, other_ref, local_sem, send_sem, recv_sem,
                    pair_sem):
    zl = lax.axis_index("zl")
    c = lax.axis_index("core")
    me = lax.axis_index("zh") * nxy + lax.axis_index("xy")

    def peer(b):
        return (zl, c, b // nxy, lax.rem(b, nxy))

    barrier = pltpu.get_barrier_semaphore()

    def greet(p, carry):
        pl.semaphore_signal(barrier, 1, device_id=peer(lax.rem(me + p, nb)), device_id_type=MESH)
        return carry

    lax.fori_loop(1, nb, greet, 0)
    pl.semaphore_wait(barrier, nb - 1)

    mine = pltpu.make_async_copy(src_ref.at[me], out_ref.at[me], local_sem)
    mine.start()

    def copy(p, dest):
        return pltpu.make_async_remote_copy(
            src_ref=src_ref.at[dest],
            dst_ref=out_ref.at[me],
            send_sem=send_sem.at[p],
            recv_sem=recv_sem.at[me],
            device_id=peer(dest),
            device_id_type=MESH,
        )

    def send(p, carry):
        copy(p, lax.rem(me + p, nb)).start()
        return carry

    lax.fori_loop(1, nb, send, 0)

    twin = lax.rem(me + nb // 2, nb)
    pair_copy = pltpu.make_async_remote_copy(
        src_ref=mine_ref,
        dst_ref=other_ref,
        send_sem=pair_sem.at[0],
        recv_sem=pair_sem.at[1],
        device_id=peer(twin),
        device_id_type=MESH,
    )
    pair_copy.start()

    def receive(p, carry):
        source = lax.rem(me + nb - p, nb)
        pltpu.make_async_remote_copy(
            src_ref=src_ref.at[source],
            dst_ref=out_ref.at[source],
            send_sem=send_sem.at[p],
            recv_sem=recv_sem.at[source],
            device_id=peer(source),
            device_id_type=MESH,
        ).wait_recv()
        return carry

    lax.fori_loop(1, nb, receive, 0)
    mine.wait()
    pair_copy.wait_recv()
    pair_copy.wait_send()

    def sent(p, carry):
        copy(p, lax.rem(me + p, nb)).wait_send()
        return carry

    lax.fori_loop(1, nb, sent, 0)


def bulk_exchange(outgoing, mine_t, nb, nxy):
    return pl.pallas_call(
        functools.partial(exchange_kernel, nb, nxy),
        out_shape=(
            jax.ShapeDtypeStruct(outgoing.shape, outgoing.dtype),
            jax.ShapeDtypeStruct(mine_t.shape, mine_t.dtype),
        ),
        in_specs=[pl.BlockSpec(memory_space=pltpu.VMEM)] * 2,
        out_specs=(pl.BlockSpec(memory_space=pltpu.VMEM), pl.BlockSpec(memory_space=pltpu.VMEM)),
        scratch_shapes=[
            pltpu.SemaphoreType.DMA(()),
            pltpu.SemaphoreType.DMA((nb,)),
            pltpu.SemaphoreType.DMA((nb,)),
            pltpu.SemaphoreType.DMA((2,)),
        ],
        compiler_params=pltpu.CompilerParams(collective_id=1, has_side_effects=True),
    )(outgoing, mine_t)


def local(residual_in, amplitudes, integral_tiles, tile_reader, tile_k, tile_column):
    nxy = lax.axis_size("xy")
    targets = lax.axis_size("zh") * nxy
    height, width = integral_tiles.shape[1], integral_tiles.shape[2]
    filled, local_index, slot_position = bucket_slots(
        tile_reader, tile_k, tile_column, targets, SLOT
    )
    picked = jnp.take(integral_tiles, local_index.reshape(-1), axis=0)
    picked = jnp.where(filled.reshape(-1)[:, None, None] > 0, picked, 0.0)
    label = jnp.zeros((targets, 1, width), jnp.float32).at[:, 0, :SLOT].set(
        slot_position.reshape(targets, SLOT).astype(jnp.float32)
    )
    outgoing = jnp.concatenate([picked.reshape(targets, SLOT * height, width), label], axis=1)
    arrived, other_t = bulk_exchange(outgoing, amplitudes.T, targets, nxy)
    position = arrived[:, SLOT * height, :SLOT].reshape(-1).astype(jnp.int32)
    arrived = arrived[:, : SLOT * height, :].reshape(targets * SLOT, height * width)
    table = (position[None, :] == jnp.arange(KT * CT, dtype=jnp.int32)[:, None]).astype(jnp.float32)
    placed = jnp.dot(table, arrived, precision=lax.Precision.HIGHEST)
    placed = placed.reshape(KT, CT, height, width).transpose(0, 2, 1, 3).reshape(KT * height, CT * width)
    nz = lax.axis_size("zl")
    gathered = row_gather(placed, nz)
    dense = gathered.reshape(-1, CT * width)
    other = other_t.T
    lower = lax.axis_index("zh") == 0
    pair = jnp.stack([jnp.where(lower, amplitudes, other), jnp.where(lower, other, amplitudes)])
    blocks = lax.all_gather(pair, "xy", axis=0, tiled=False)
    rows, own_cols = amplitudes.shape
    amps = blocks.transpose(2, 1, 0, 3).reshape(rows, targets * own_cols)
    groups = gathered.shape[0]
    amps = amps.reshape(rows, KT, groups, height).transpose(0, 2, 1, 3).reshape(rows, -1)
    return residual_in + jnp.dot(amps, dense, precision=lax.Precision.HIGH)


def solution(mesh):
    row_size = mesh.shape["row"]
    bulk_size = mesh.shape["bulk"]
    devices = np.asarray(mesh.devices).reshape(row_size // 2, 2, Z_HALVES, bulk_size // Z_HALVES)
    inner = Mesh(devices, ("zl", "core", "zh", "xy"))
    row = ("zl", "core")
    bulk = ("zh", "xy")
    placed = (
        P(row, bulk),
        P(row, bulk),
        P(bulk, row, None),
        P(bulk, None),
        P(bulk),
        P(bulk),
    )
    return jax.shard_map(
        local, mesh=inner, in_specs=placed, out_specs=P(row, bulk), check_vma=False
    )
```

```python
import functools

import jax
import jax.numpy as jnp
import numpy as np
from jax import lax
from jax.experimental import pallas as pl
from jax.experimental.pallas import tpu as pltpu
from jax.sharding import Mesh, PartitionSpec as P

MESH = pl.DeviceIdType.MESH

KT = 16
CT = 8
SLOT = 2
Z_HALVES = 2
RELAY_PARTS = 4


def bucket_slots(tile_reader, tile_k, tile_column, targets, slots):
    readers = tile_reader[:, 0]
    matches = (readers[:, None] == jnp.arange(targets, dtype=jnp.int32)[None, :]).astype(jnp.int32)
    ordinal = jnp.cumsum(matches, axis=0) - matches
    position = jnp.sum(ordinal * matches, axis=1)
    select = matches.T[:, None, :] * (
        position[None, None, :] == jnp.arange(slots, dtype=jnp.int32)[None, :, None]
    ).astype(jnp.int32)
    filled = jnp.sum(select, axis=2)
    local_index = jnp.sum(select * jnp.arange(readers.shape[0], dtype=jnp.int32)[None, None, :], axis=2)
    slot_position = jnp.sum(select * (tile_k * CT + tile_column)[None, None, :], axis=2) + filled - 1
    return filled, local_index, slot_position


def gather_kernel(nz, parts, src_ref, out_ref, local_sem, send_sem, recv_sem):
    zl = lax.axis_index("zl")
    c = lax.axis_index("core")
    zh = lax.axis_index("zh")
    xy = lax.axis_index("xy")
    partner = (zl, 1 - c, zh, xy)
    left = (zl - 1, c, zh, xy)
    right = (zl + 1, c, zh, xy)
    has_left = zl > 0
    has_right = zl < nz - 1
    own = zl * 2 + c

    barrier = pltpu.get_barrier_semaphore()
    pl.semaphore_signal(barrier, 1, device_id=partner, device_id_type=MESH)

    @pl.when(has_left)
    def _():
        pl.semaphore_signal(barrier, 1, device_id=left, device_id_type=MESH)

    @pl.when(has_right)
    def _():
        pl.semaphore_signal(barrier, 1, device_id=right, device_id_type=MESH)

    peers = 1 + has_left.astype(jnp.int32) + has_right.astype(jnp.int32)
    pl.semaphore_wait(barrier, peers)

    piece = src_ref.shape[0] // parts

    def copy(src, slot, kind, dev, q):
        rows = pl.ds(q * piece, piece)
        return pltpu.make_async_remote_copy(
            src_ref=src.at[rows],
            dst_ref=out_ref.at[slot, rows],
            send_sem=send_sem.at[slot, q, kind],
            recv_sem=recv_sem.at[slot, q],
            device_id=dev,
            device_id_type=MESH,
        )

    mine = pltpu.make_async_copy(src_ref, out_ref.at[own], local_sem)
    mine.start()
    for q in range(parts):
        copy(src_ref, own, 0, partner, q).start()

        @pl.when(has_left)
        def _():
            copy(src_ref, own, 1, left, q).start()

        @pl.when(has_right)
        def _():
            copy(src_ref, own, 2, right, q).start()

    for d in range(1, nz):
        for q in range(parts):
            @pl.when(zl - d >= 0)
            def _():
                s = (zl - d) * 2 + c
                copy(out_ref.at[s], s, 0, partner, q).wait_recv()
                copy(out_ref.at[s], s, 0, partner, q).start()

                @pl.when(has_right)
                def _():
                    copy(out_ref.at[s], s, 2, right, q).start()

            @pl.when(zl + d <= nz - 1)
            def _():
                s = (zl + d) * 2 + c
                copy(out_ref.at[s], s, 0, partner, q).wait_recv()
                copy(out_ref.at[s], s, 0, partner, q).start()

                @pl.when(has_left)
                def _():
                    copy(out_ref.at[s], s, 1, left, q).start()

    for z in range(nz):
        s = z * 2 + (1 - c)
        for q in range(parts):
            copy(out_ref.at[s], s, 0, partner, q).wait_recv()

    mine.wait()
    for z in range(nz):
        s = z * 2 + c
        for q in range(parts):
            copy(out_ref.at[s], s, 0, partner, q).wait_send()

            @pl.when(has_left & (z >= zl))
            def _():
                copy(out_ref.at[s], s, 1, left, q).wait_send()

            @pl.when(has_right & (z <= zl))
            def _():
                copy(out_ref.at[s], s, 2, right, q).wait_send()


def row_gather(placed, nz):
    groups = 2 * nz
    return pl.pallas_call(
        functools.partial(gather_kernel, nz, RELAY_PARTS),
        out_shape=jax.ShapeDtypeStruct((groups,) + placed.shape, placed.dtype),
        in_specs=[pl.BlockSpec(memory_space=pltpu.VMEM)],
        out_specs=pl.BlockSpec(memory_space=pltpu.VMEM),
        scratch_shapes=[
            pltpu.SemaphoreType.DMA(()),
            pltpu.SemaphoreType.DMA((groups, RELAY_PARTS, 3)),
            pltpu.SemaphoreType.DMA((groups, RELAY_PARTS)),
        ],
        compiler_params=pltpu.CompilerParams(collective_id=0, has_side_effects=True),
    )(placed)


def exchange_kernel(nb, nxy, src_ref, mine_ref, out_ref, other_ref, local_sem, send_sem, recv_sem,
                    pair_sem):
    zl = lax.axis_index("zl")
    c = lax.axis_index("core")
    me = lax.axis_index("zh") * nxy + lax.axis_index("xy")

    def peer(b):
        return (zl, c, b // nxy, lax.rem(b, nxy))

    barrier = pltpu.get_barrier_semaphore()

    def greet(p, carry):
        pl.semaphore_signal(barrier, 1, device_id=peer(lax.rem(me + p, nb)), device_id_type=MESH)
        return carry

    lax.fori_loop(1, nb, greet, 0)
    pl.semaphore_wait(barrier, nb - 1)

    mine = pltpu.make_async_copy(src_ref.at[me], out_ref.at[me], local_sem)
    mine.start()

    def copy(p, dest):
        return pltpu.make_async_remote_copy(
            src_ref=src_ref.at[dest],
            dst_ref=out_ref.at[me],
            send_sem=send_sem.at[p],
            recv_sem=recv_sem.at[me],
            device_id=peer(dest),
            device_id_type=MESH,
        )

    def send(p, carry):
        copy(p, lax.rem(me + p, nb)).start()
        return carry

    lax.fori_loop(1, nb, send, 0)

    twin = lax.rem(me + nb // 2, nb)
    pair_copy = pltpu.make_async_remote_copy(
        src_ref=mine_ref,
        dst_ref=other_ref,
        send_sem=pair_sem.at[0],
        recv_sem=pair_sem.at[1],
        device_id=peer(twin),
        device_id_type=MESH,
    )
    pair_copy.start()

    def receive(p, carry):
        source = lax.rem(me + nb - p, nb)
        pltpu.make_async_remote_copy(
            src_ref=src_ref.at[source],
            dst_ref=out_ref.at[source],
            send_sem=send_sem.at[p],
            recv_sem=recv_sem.at[source],
            device_id=peer(source),
            device_id_type=MESH,
        ).wait_recv()
        return carry

    lax.fori_loop(1, nb, receive, 0)
    mine.wait()
    pair_copy.wait_recv()
    pair_copy.wait_send()

    def sent(p, carry):
        copy(p, lax.rem(me + p, nb)).wait_send()
        return carry

    lax.fori_loop(1, nb, sent, 0)


def bulk_exchange(outgoing, mine_t, nb, nxy):
    return pl.pallas_call(
        functools.partial(exchange_kernel, nb, nxy),
        out_shape=(
            jax.ShapeDtypeStruct(outgoing.shape, outgoing.dtype),
            jax.ShapeDtypeStruct(mine_t.shape, mine_t.dtype),
        ),
        in_specs=[pl.BlockSpec(memory_space=pltpu.VMEM)] * 2,
        out_specs=(pl.BlockSpec(memory_space=pltpu.VMEM), pl.BlockSpec(memory_space=pltpu.VMEM)),
        scratch_shapes=[
            pltpu.SemaphoreType.DMA(()),
            pltpu.SemaphoreType.DMA((nb,)),
            pltpu.SemaphoreType.DMA((nb,)),
            pltpu.SemaphoreType.DMA((2,)),
        ],
        compiler_params=pltpu.CompilerParams(collective_id=1, has_side_effects=True),
    )(outgoing, mine_t)


def local(residual_in, amplitudes, integral_tiles, tile_reader, tile_k, tile_column):
    nxy = lax.axis_size("xy")
    targets = lax.axis_size("zh") * nxy
    height, width = integral_tiles.shape[1], integral_tiles.shape[2]
    filled, local_index, slot_position = bucket_slots(
        tile_reader, tile_k, tile_column, targets, SLOT
    )
    picked = jnp.take(integral_tiles, local_index.reshape(-1), axis=0)
    picked = jnp.where(filled.reshape(-1)[:, None, None] > 0, picked, 0.0)
    label = jnp.zeros((targets, 1, width), jnp.float32).at[:, 0, :SLOT].set(
        slot_position.reshape(targets, SLOT).astype(jnp.float32)
    )
    outgoing = jnp.concatenate([picked.reshape(targets, SLOT * height, width), label], axis=1)
    arrived, other_t = bulk_exchange(outgoing, amplitudes.T, targets, nxy)
    position = arrived[:, SLOT * height, :SLOT].reshape(-1).astype(jnp.int32)
    arrived = arrived[:, : SLOT * height, :].reshape(targets * SLOT, height * width)
    table = (position[None, :] == jnp.arange(KT * CT, dtype=jnp.int32)[:, None]).astype(jnp.float32)
    placed = jnp.dot(table, arrived, precision=lax.Precision.HIGHEST)
    placed = placed.reshape(KT, CT, height, width).transpose(0, 2, 1, 3).reshape(KT * height, CT * width)
    nz = lax.axis_size("zl")
    gathered = row_gather(placed, nz)
    dense = gathered.reshape(-1, CT * width)
    other = other_t.T
    lower = lax.axis_index("zh") == 0
    pair = jnp.stack([jnp.where(lower, amplitudes, other), jnp.where(lower, other, amplitudes)])
    blocks = lax.all_gather(pair, "xy", axis=0, tiled=False)
    rows, own_cols = amplitudes.shape
    amps = blocks.transpose(2, 1, 0, 3).reshape(rows, targets * own_cols)
    groups = gathered.shape[0]
    amps = amps.reshape(rows, KT, groups, height).transpose(0, 2, 1, 3).reshape(rows, -1)
    return residual_in + jnp.dot(amps, dense, precision=lax.Precision.HIGH)


def solution(mesh):
    row_size = mesh.shape["row"]
    bulk_size = mesh.shape["bulk"]
    devices = np.asarray(mesh.devices).reshape(row_size // 2, 2, Z_HALVES, bulk_size // Z_HALVES)
    inner = Mesh(devices, ("zl", "core", "zh", "xy"))
    row = ("zl", "core")
    bulk = ("zh", "xy")
    placed = (
        P(row, bulk),
        P(row, bulk),
        P(bulk, row, None),
        P(bulk, None),
        P(bulk),
        P(bulk),
    )
    return jax.shard_map(
        local, mesh=inner, in_specs=placed, out_specs=P(row, bulk), check_vma=False
    )
```

```python
import functools

import jax
import jax.numpy as jnp
import numpy as np
from jax import lax
from jax.experimental import pallas as pl
from jax.experimental.pallas import tpu as pltpu
from jax.sharding import Mesh, PartitionSpec as P

MESH = pl.DeviceIdType.MESH

KT = 16
CT = 8
SLOT = 2
Z_HALVES = 2
RELAY_PARTS = 2


def bucket_slots(tile_reader, tile_k, tile_column, targets, slots):
    readers = tile_reader[:, 0]
    matches = (readers[:, None] == jnp.arange(targets, dtype=jnp.int32)[None, :]).astype(jnp.int32)
    ordinal = jnp.cumsum(matches, axis=0) - matches
    position = jnp.sum(ordinal * matches, axis=1)
    select = matches.T[:, None, :] * (
        position[None, None, :] == jnp.arange(slots, dtype=jnp.int32)[None, :, None]
    ).astype(jnp.int32)
    filled = jnp.sum(select, axis=2)
    local_index = jnp.sum(select * jnp.arange(readers.shape[0], dtype=jnp.int32)[None, None, :], axis=2)
    slot_position = jnp.sum(select * (tile_k * CT + tile_column)[None, None, :], axis=2) + filled - 1
    return filled, local_index, slot_position


def gather_kernel(nz, parts, src_ref, out_ref, local_sem, send_sem, recv_sem):
    zl = lax.axis_index("zl")
    c = lax.axis_index("core")
    zh = lax.axis_index("zh")
    xy = lax.axis_index("xy")
    partner = (zl, 1 - c, zh, xy)
    left = (zl - 1, c, zh, xy)
    right = (zl + 1, c, zh, xy)
    has_left = zl > 0
    has_right = zl < nz - 1
    own = zl * 2 + c

    barrier = pltpu.get_barrier_semaphore()
    pl.semaphore_signal(barrier, 1, device_id=partner, device_id_type=MESH)

    @pl.when(has_left)
    def _():
        pl.semaphore_signal(barrier, 1, device_id=left, device_id_type=MESH)

    @pl.when(has_right)
    def _():
        pl.semaphore_signal(barrier, 1, device_id=right, device_id_type=MESH)

    peers = 1 + has_left.astype(jnp.int32) + has_right.astype(jnp.int32)
    pl.semaphore_wait(barrier, peers)

    piece = src_ref.shape[0] // parts

    def copy(src, slot, kind, dev, q):
        rows = pl.ds(q * piece, piece)
        return pltpu.make_async_remote_copy(
            src_ref=src.at[rows],
            dst_ref=out_ref.at[slot, rows],
            send_sem=send_sem.at[slot, q, kind],
            recv_sem=recv_sem.at[slot, q],
            device_id=dev,
            device_id_type=MESH,
        )

    mine = pltpu.make_async_copy(src_ref, out_ref.at[own], local_sem)
    mine.start()
    for q in range(parts):
        copy(src_ref, own, 0, partner, q).start()

        @pl.when(has_left)
        def _():
            copy(src_ref, own, 1, left, q).start()

        @pl.when(has_right)
        def _():
            copy(src_ref, own, 2, right, q).start()

    for d in range(1, nz):
        for q in range(parts):
            @pl.when(zl - d >= 0)
            def _():
                s = (zl - d) * 2 + c
                copy(out_ref.at[s], s, 0, partner, q).wait_recv()
                copy(out_ref.at[s], s, 0, partner, q).start()

                @pl.when(has_right)
                def _():
                    copy(out_ref.at[s], s, 2, right, q).start()

            @pl.when(zl + d <= nz - 1)
            def _():
                s = (zl + d) * 2 + c
                copy(out_ref.at[s], s, 0, partner, q).wait_recv()
                copy(out_ref.at[s], s, 0, partner, q).start()

                @pl.when(has_left)
                def _():
                    copy(out_ref.at[s], s, 1, left, q).start()

    for z in range(nz):
        s = z * 2 + (1 - c)
        for q in range(parts):
            copy(out_ref.at[s], s, 0, partner, q).wait_recv()

    mine.wait()
    for z in range(nz):
        s = z * 2 + c
        for q in range(parts):
            copy(out_ref.at[s], s, 0, partner, q).wait_send()

            @pl.when(has_left & (z >= zl))
            def _():
                copy(out_ref.at[s], s, 1, left, q).wait_send()

            @pl.when(has_right & (z <= zl))
            def _():
                copy(out_ref.at[s], s, 2, right, q).wait_send()


def row_gather(placed, nz):
    groups = 2 * nz
    return pl.pallas_call(
        functools.partial(gather_kernel, nz, RELAY_PARTS),
        out_shape=jax.ShapeDtypeStruct((groups,) + placed.shape, placed.dtype),
        in_specs=[pl.BlockSpec(memory_space=pltpu.VMEM)],
        out_specs=pl.BlockSpec(memory_space=pltpu.VMEM),
        scratch_shapes=[
            pltpu.SemaphoreType.DMA(()),
            pltpu.SemaphoreType.DMA((groups, RELAY_PARTS, 3)),
            pltpu.SemaphoreType.DMA((groups, RELAY_PARTS)),
        ],
        compiler_params=pltpu.CompilerParams(collective_id=0, has_side_effects=True),
    )(placed)


def exchange_kernel(nb, nxy, src_ref, mine_ref, out_ref, other_ref, local_sem, send_sem, recv_sem,
                    pair_sem):
    zl = lax.axis_index("zl")
    c = lax.axis_index("core")
    me = lax.axis_index("zh") * nxy + lax.axis_index("xy")

    def peer(b):
        return (zl, c, b // nxy, lax.rem(b, nxy))

    barrier = pltpu.get_barrier_semaphore()

    def greet(p, carry):
        pl.semaphore_signal(barrier, 1, device_id=peer(lax.rem(me + p, nb)), device_id_type=MESH)
        return carry

    lax.fori_loop(1, nb, greet, 0)
    pl.semaphore_wait(barrier, nb - 1)

    mine = pltpu.make_async_copy(src_ref.at[me], out_ref.at[me], local_sem)
    mine.start()

    def copy(p, dest):
        return pltpu.make_async_remote_copy(
            src_ref=src_ref.at[dest],
            dst_ref=out_ref.at[me],
            send_sem=send_sem.at[p],
            recv_sem=recv_sem.at[me],
            device_id=peer(dest),
            device_id_type=MESH,
        )

    def send(p, carry):
        copy(p, lax.rem(me + p, nb)).start()
        return carry

    lax.fori_loop(1, nb, send, 0)

    twin = lax.rem(me + nb // 2, nb)
    pair_copy = pltpu.make_async_remote_copy(
        src_ref=mine_ref,
        dst_ref=other_ref,
        send_sem=pair_sem.at[0],
        recv_sem=pair_sem.at[1],
        device_id=peer(twin),
        device_id_type=MESH,
    )
    pair_copy.start()

    def receive(p, carry):
        source = lax.rem(me + nb - p, nb)
        pltpu.make_async_remote_copy(
            src_ref=src_ref.at[source],
            dst_ref=out_ref.at[source],
            send_sem=send_sem.at[p],
            recv_sem=recv_sem.at[source],
            device_id=peer(source),
            device_id_type=MESH,
        ).wait_recv()
        return carry

    lax.fori_loop(1, nb, receive, 0)
    mine.wait()
    pair_copy.wait_recv()
    pair_copy.wait_send()

    def sent(p, carry):
        copy(p, lax.rem(me + p, nb)).wait_send()
        return carry

    lax.fori_loop(1, nb, sent, 0)


def bulk_exchange(outgoing, mine_t, nb, nxy):
    return pl.pallas_call(
        functools.partial(exchange_kernel, nb, nxy),
        out_shape=(
            jax.ShapeDtypeStruct(outgoing.shape, outgoing.dtype),
            jax.ShapeDtypeStruct(mine_t.shape, mine_t.dtype),
        ),
        in_specs=[pl.BlockSpec(memory_space=pltpu.VMEM)] * 2,
        out_specs=(pl.BlockSpec(memory_space=pltpu.VMEM), pl.BlockSpec(memory_space=pltpu.VMEM)),
        scratch_shapes=[
            pltpu.SemaphoreType.DMA(()),
            pltpu.SemaphoreType.DMA((nb,)),
            pltpu.SemaphoreType.DMA((nb,)),
            pltpu.SemaphoreType.DMA((2,)),
        ],
        compiler_params=pltpu.CompilerParams(collective_id=1, has_side_effects=True),
    )(outgoing, mine_t)


def local(residual_in, amplitudes, integral_tiles, tile_reader, tile_k, tile_column):
    nxy = lax.axis_size("xy")
    targets = lax.axis_size("zh") * nxy
    height, width = integral_tiles.shape[1], integral_tiles.shape[2]
    filled, local_index, slot_position = bucket_slots(
        tile_reader, tile_k, tile_column, targets, SLOT
    )
    picked = jnp.take(integral_tiles, local_index.reshape(-1), axis=0)
    picked = jnp.where(filled.reshape(-1)[:, None, None] > 0, picked, 0.0)
    label = jnp.zeros((targets, 1, width), jnp.float32).at[:, 0, :SLOT].set(
        slot_position.reshape(targets, SLOT).astype(jnp.float32)
    )
    outgoing = jnp.concatenate([picked.reshape(targets, SLOT * height, width), label], axis=1)
    arrived, other_t = bulk_exchange(outgoing, amplitudes.T, targets, nxy)
    position = arrived[:, SLOT * height, :SLOT].reshape(-1).astype(jnp.int32)
    arrived = arrived[:, : SLOT * height, :].reshape(targets * SLOT, height * width)
    table = (position[None, :] == jnp.arange(KT * CT, dtype=jnp.int32)[:, None]).astype(jnp.float32)
    placed = jnp.dot(table, arrived, precision=lax.Precision.HIGHEST)
    placed = placed.reshape(KT, CT, height, width).transpose(0, 2, 1, 3).reshape(KT * height, CT * width)
    nz = lax.axis_size("zl")
    gathered = row_gather(placed, nz)
    dense = gathered.reshape(-1, CT * width)
    near = lax.all_gather(amplitudes, "xy", axis=0, tiled=False)
    far = lax.all_gather(other_t.T, "xy", axis=0, tiled=False)
    lower = lax.axis_index("zh") == 0
    blocks = jnp.stack([jnp.where(lower, near, far), jnp.where(lower, far, near)], axis=1)
    rows, own_cols = amplitudes.shape
    amps = blocks.transpose(2, 1, 0, 3).reshape(rows, targets * own_cols)
    groups = gathered.shape[0]
    amps = amps.reshape(rows, KT, groups, height).transpose(0, 2, 1, 3).reshape(rows, -1)
    return residual_in + jnp.dot(amps, dense, precision=lax.Precision.HIGH)


def solution(mesh):
    row_size = mesh.shape["row"]
    bulk_size = mesh.shape["bulk"]
    devices = np.asarray(mesh.devices).reshape(row_size // 2, 2, Z_HALVES, bulk_size // Z_HALVES)
    inner = Mesh(devices, ("zl", "core", "zh", "xy"))
    row = ("zl", "core")
    bulk = ("zh", "xy")
    placed = (
        P(row, bulk),
        P(row, bulk),
        P(bulk, row, None),
        P(bulk, None),
        P(bulk),
        P(bulk),
    )
    return jax.shard_map(
        local, mesh=inner, in_specs=placed, out_specs=P(row, bulk), check_vma=False
    )
```

```python
import functools

import jax
import jax.numpy as jnp
import numpy as np
from jax import lax
from jax.experimental import pallas as pl
from jax.experimental.pallas import tpu as pltpu
from jax.sharding import Mesh, PartitionSpec as P

MESH = pl.DeviceIdType.MESH

KT = 16
CT = 8
SLOT = 2
Z_HALVES = 2
RELAY_PARTS = 2


def bucket_slots(tile_reader, tile_k, tile_column, targets, slots):
    readers = tile_reader[:, 0]
    matches = (readers[:, None] == jnp.arange(targets, dtype=jnp.int32)[None, :]).astype(jnp.int32)
    ordinal = jnp.cumsum(matches, axis=0) - matches
    position = jnp.sum(ordinal * matches, axis=1)
    select = matches.T[:, None, :] * (
        position[None, None, :] == jnp.arange(slots, dtype=jnp.int32)[None, :, None]
    ).astype(jnp.int32)
    filled = jnp.sum(select, axis=2)
    local_index = jnp.sum(select * jnp.arange(readers.shape[0], dtype=jnp.int32)[None, None, :], axis=2)
    slot_position = jnp.sum(select * (tile_k * CT + tile_column)[None, None, :], axis=2) + filled - 1
    return filled, local_index, slot_position


def gather_kernel(nz, parts, src_ref, out_ref, local_sem, send_sem, recv_sem):
    zl = lax.axis_index("zl")
    c = lax.axis_index("core")
    zh = lax.axis_index("zh")
    xy = lax.axis_index("xy")
    partner = (zl, 1 - c, zh, xy)
    left = (zl - 1, c, zh, xy)
    right = (zl + 1, c, zh, xy)
    has_left = zl > 0
    has_right = zl < nz - 1
    own = zl * 2 + c

    barrier = pltpu.get_barrier_semaphore()
    pl.semaphore_signal(barrier, 1, device_id=partner, device_id_type=MESH)

    @pl.when(has_left)
    def _():
        pl.semaphore_signal(barrier, 1, device_id=left, device_id_type=MESH)

    @pl.when(has_right)
    def _():
        pl.semaphore_signal(barrier, 1, device_id=right, device_id_type=MESH)

    peers = 1 + has_left.astype(jnp.int32) + has_right.astype(jnp.int32)
    pl.semaphore_wait(barrier, peers)

    piece = src_ref.shape[0] // parts

    def copy(src, slot, kind, dev, q):
        rows = pl.ds(q * piece, piece)
        return pltpu.make_async_remote_copy(
            src_ref=src.at[rows],
            dst_ref=out_ref.at[rows, slot],
            send_sem=send_sem.at[slot, q, kind],
            recv_sem=recv_sem.at[slot, q],
            device_id=dev,
            device_id_type=MESH,
        )

    mine = pltpu.make_async_copy(src_ref, out_ref.at[:, own], local_sem)
    mine.start()
    for q in range(parts):
        copy(src_ref, own, 0, partner, q).start()

        @pl.when(has_left)
        def _():
            copy(src_ref, own, 1, left, q).start()

        @pl.when(has_right)
        def _():
            copy(src_ref, own, 2, right, q).start()

    for d in range(1, nz):
        for q in range(parts):
            @pl.when(zl - d >= 0)
            def _():
                s = (zl - d) * 2 + c
                copy(out_ref.at[:, s], s, 0, partner, q).wait_recv()
                copy(out_ref.at[:, s], s, 0, partner, q).start()

                @pl.when(has_right)
                def _():
                    copy(out_ref.at[:, s], s, 2, right, q).start()

            @pl.when(zl + d <= nz - 1)
            def _():
                s = (zl + d) * 2 + c
                copy(out_ref.at[:, s], s, 0, partner, q).wait_recv()
                copy(out_ref.at[:, s], s, 0, partner, q).start()

                @pl.when(has_left)
                def _():
                    copy(out_ref.at[:, s], s, 1, left, q).start()

    for z in range(nz):
        s = z * 2 + (1 - c)
        for q in range(parts):
            copy(out_ref.at[:, s], s, 0, partner, q).wait_recv()

    mine.wait()
    for z in range(nz):
        s = z * 2 + c
        for q in range(parts):
            copy(out_ref.at[:, s], s, 0, partner, q).wait_send()

            @pl.when(has_left & (z >= zl))
            def _():
                copy(out_ref.at[:, s], s, 1, left, q).wait_send()

            @pl.when(has_right & (z <= zl))
            def _():
                copy(out_ref.at[:, s], s, 2, right, q).wait_send()


def row_gather(placed, nz):
    groups = 2 * nz
    return pl.pallas_call(
        functools.partial(gather_kernel, nz, RELAY_PARTS),
        out_shape=jax.ShapeDtypeStruct(placed.shape[:1] + (groups,) + placed.shape[1:], placed.dtype),
        in_specs=[pl.BlockSpec(memory_space=pltpu.VMEM)],
        out_specs=pl.BlockSpec(memory_space=pltpu.VMEM),
        scratch_shapes=[
            pltpu.SemaphoreType.DMA(()),
            pltpu.SemaphoreType.DMA((groups, RELAY_PARTS, 3)),
            pltpu.SemaphoreType.DMA((groups, RELAY_PARTS)),
        ],
        compiler_params=pltpu.CompilerParams(collective_id=0, has_side_effects=True),
    )(placed)


def exchange_kernel(nb, nxy, src_ref, mine_ref, out_ref, other_ref, local_sem, send_sem, recv_sem,
                    pair_sem):
    zl = lax.axis_index("zl")
    c = lax.axis_index("core")
    me = lax.axis_index("zh") * nxy + lax.axis_index("xy")

    def peer(b):
        return (zl, c, b // nxy, lax.rem(b, nxy))

    barrier = pltpu.get_barrier_semaphore()

    def greet(p, carry):
        pl.semaphore_signal(barrier, 1, device_id=peer(lax.rem(me + p, nb)), device_id_type=MESH)
        return carry

    lax.fori_loop(1, nb, greet, 0)
    pl.semaphore_wait(barrier, nb - 1)

    mine = pltpu.make_async_copy(src_ref.at[me], out_ref.at[me], local_sem)
    mine.start()

    def copy(p, dest):
        return pltpu.make_async_remote_copy(
            src_ref=src_ref.at[dest],
            dst_ref=out_ref.at[me],
            send_sem=send_sem.at[p],
            recv_sem=recv_sem.at[me],
            device_id=peer(dest),
            device_id_type=MESH,
        )

    def send(p, carry):
        copy(p, lax.rem(me + p, nb)).start()
        return carry

    lax.fori_loop(1, nb, send, 0)

    twin = lax.rem(me + nb // 2, nb)
    pair_copy = pltpu.make_async_remote_copy(
        src_ref=mine_ref,
        dst_ref=other_ref,
        send_sem=pair_sem.at[0],
        recv_sem=pair_sem.at[1],
        device_id=peer(twin),
        device_id_type=MESH,
    )
    pair_copy.start()

    def receive(p, carry):
        source = lax.rem(me + nb - p, nb)
        pltpu.make_async_remote_copy(
            src_ref=src_ref.at[source],
            dst_ref=out_ref.at[source],
            send_sem=send_sem.at[p],
            recv_sem=recv_sem.at[source],
            device_id=peer(source),
            device_id_type=MESH,
        ).wait_recv()
        return carry

    lax.fori_loop(1, nb, receive, 0)
    mine.wait()
    pair_copy.wait_recv()
    pair_copy.wait_send()

    def sent(p, carry):
        copy(p, lax.rem(me + p, nb)).wait_send()
        return carry

    lax.fori_loop(1, nb, sent, 0)


def bulk_exchange(outgoing, mine_t, nb, nxy):
    return pl.pallas_call(
        functools.partial(exchange_kernel, nb, nxy),
        out_shape=(
            jax.ShapeDtypeStruct(outgoing.shape, outgoing.dtype),
            jax.ShapeDtypeStruct(mine_t.shape, mine_t.dtype),
        ),
        in_specs=[pl.BlockSpec(memory_space=pltpu.VMEM)] * 2,
        out_specs=(pl.BlockSpec(memory_space=pltpu.VMEM), pl.BlockSpec(memory_space=pltpu.VMEM)),
        scratch_shapes=[
            pltpu.SemaphoreType.DMA(()),
            pltpu.SemaphoreType.DMA((nb,)),
            pltpu.SemaphoreType.DMA((nb,)),
            pltpu.SemaphoreType.DMA((2,)),
        ],
        compiler_params=pltpu.CompilerParams(collective_id=1, has_side_effects=True),
    )(outgoing, mine_t)


def local(residual_in, amplitudes, integral_tiles, tile_reader, tile_k, tile_column):
    nxy = lax.axis_size("xy")
    targets = lax.axis_size("zh") * nxy
    height, width = integral_tiles.shape[1], integral_tiles.shape[2]
    filled, local_index, slot_position = bucket_slots(
        tile_reader, tile_k, tile_column, targets, SLOT
    )
    picked = jnp.take(integral_tiles, local_index.reshape(-1), axis=0)
    picked = jnp.where(filled.reshape(-1)[:, None, None] > 0, picked, 0.0)
    label = jnp.zeros((targets, 1, width), jnp.float32).at[:, 0, :SLOT].set(
        slot_position.reshape(targets, SLOT).astype(jnp.float32)
    )
    outgoing = jnp.concatenate([picked.reshape(targets, SLOT * height, width), label], axis=1)
    arrived, other_t = bulk_exchange(outgoing, amplitudes.T, targets, nxy)
    position = arrived[:, SLOT * height, :SLOT].reshape(-1).astype(jnp.int32)
    arrived = arrived[:, : SLOT * height, :].reshape(targets * SLOT, height * width)
    table = (position[None, :] == jnp.arange(KT * CT, dtype=jnp.int32)[:, None]).astype(jnp.float32)
    placed = jnp.dot(table, arrived, precision=lax.Precision.HIGHEST)
    placed = placed.reshape(KT, CT, height, width).transpose(0, 2, 1, 3).reshape(KT, height, CT * width)
    nz = lax.axis_size("zl")
    gathered = row_gather(placed, nz)
    dense = gathered.reshape(-1, CT * width)
    other = other_t.T
    lower = lax.axis_index("zh") == 0
    pair = jnp.stack([jnp.where(lower, amplitudes, other), jnp.where(lower, other, amplitudes)])
    blocks = lax.all_gather(pair, "xy", axis=0, tiled=False)
    rows, own_cols = amplitudes.shape
    amps = blocks.transpose(2, 1, 0, 3).reshape(rows, targets * own_cols)
    return residual_in + jnp.dot(amps, dense, precision=lax.Precision.HIGH)


def solution(mesh):
    row_size = mesh.shape["row"]
    bulk_size = mesh.shape["bulk"]
    devices = np.asarray(mesh.devices).reshape(row_size // 2, 2, Z_HALVES, bulk_size // Z_HALVES)
    inner = Mesh(devices, ("zl", "core", "zh", "xy"))
    row = ("zl", "core")
    bulk = ("zh", "xy")
    placed = (
        P(row, bulk),
        P(row, bulk),
        P(bulk, row, None),
        P(bulk, None),
        P(bulk),
        P(bulk),
    )
    return jax.shard_map(
        local, mesh=inner, in_specs=placed, out_specs=P(row, bulk), check_vma=False
    )
```

```python
import functools

import jax
import jax.numpy as jnp
import numpy as np
from jax import lax
from jax.experimental import pallas as pl
from jax.experimental.pallas import tpu as pltpu
from jax.sharding import Mesh, PartitionSpec as P

MESH = pl.DeviceIdType.MESH

KT = 16
CT = 8
SLOT = 2
Z_HALVES = 2
RELAY_PARTS = 2


def bucket_slots(tile_reader, tile_k, tile_column, targets, slots):
    readers = tile_reader[:, 0]
    matches = (readers[:, None] == jnp.arange(targets, dtype=jnp.int32)[None, :]).astype(jnp.int32)
    ordinal = jnp.cumsum(matches, axis=0) - matches
    position = jnp.sum(ordinal * matches, axis=1)
    select = matches.T[:, None, :] * (
        position[None, None, :] == jnp.arange(slots, dtype=jnp.int32)[None, :, None]
    ).astype(jnp.int32)
    filled = jnp.sum(select, axis=2)
    local_index = jnp.sum(select * jnp.arange(readers.shape[0], dtype=jnp.int32)[None, None, :], axis=2)
    slot_position = jnp.sum(select * (tile_k * CT + tile_column)[None, None, :], axis=2) + filled - 1
    return filled, local_index, slot_position


def gather_kernel(nz, parts, src_ref, out_ref, local_sem, send_sem, recv_sem):
    zl = lax.axis_index("zl")
    c = lax.axis_index("core")
    zh = lax.axis_index("zh")
    xy = lax.axis_index("xy")
    partner = (zl, 1 - c, zh, xy)
    left = (zl - 1, c, zh, xy)
    right = (zl + 1, c, zh, xy)
    has_left = zl > 0
    has_right = zl < nz - 1
    own = zl * 2 + c

    barrier = pltpu.get_barrier_semaphore()
    pl.semaphore_signal(barrier, 1, device_id=partner, device_id_type=MESH)

    @pl.when(has_left)
    def _():
        pl.semaphore_signal(barrier, 1, device_id=left, device_id_type=MESH)

    @pl.when(has_right)
    def _():
        pl.semaphore_signal(barrier, 1, device_id=right, device_id_type=MESH)

    peers = 1 + has_left.astype(jnp.int32) + has_right.astype(jnp.int32)
    pl.semaphore_wait(barrier, peers)

    piece = src_ref.shape[0] // parts

    def copy(src, slot, kind, dev, q):
        rows = pl.ds(q * piece, piece)
        return pltpu.make_async_remote_copy(
            src_ref=src.at[rows],
            dst_ref=out_ref.at[slot, rows],
            send_sem=send_sem.at[slot, q, kind],
            recv_sem=recv_sem.at[slot, q],
            device_id=dev,
            device_id_type=MESH,
        )

    mine = pltpu.make_async_copy(src_ref, out_ref.at[own], local_sem)
    mine.start()
    for q in range(parts):
        copy(src_ref, own, 0, partner, q).start()

        @pl.when(has_left)
        def _():
            copy(src_ref, own, 1, left, q).start()

        @pl.when(has_right)
        def _():
            copy(src_ref, own, 2, right, q).start()

    for d in range(1, nz):
        for q in range(parts):
            @pl.when(zl - d >= 0)
            def _():
                s = (zl - d) * 2 + c
                copy(out_ref.at[s], s, 0, partner, q).wait_recv()
                copy(out_ref.at[s], s, 0, partner, q).start()

                @pl.when(has_right)
                def _():
                    copy(out_ref.at[s], s, 2, right, q).start()

            @pl.when(zl + d <= nz - 1)
            def _():
                s = (zl + d) * 2 + c
                copy(out_ref.at[s], s, 0, partner, q).wait_recv()
                copy(out_ref.at[s], s, 0, partner, q).start()

                @pl.when(has_left)
                def _():
                    copy(out_ref.at[s], s, 1, left, q).start()

    for z in range(nz):
        s = z * 2 + (1 - c)
        for q in range(parts):
            copy(out_ref.at[s], s, 0, partner, q).wait_recv()

    mine.wait()
    for z in range(nz):
        s = z * 2 + c
        for q in range(parts):
            copy(out_ref.at[s], s, 0, partner, q).wait_send()

            @pl.when(has_left & (z >= zl))
            def _():
                copy(out_ref.at[s], s, 1, left, q).wait_send()

            @pl.when(has_right & (z <= zl))
            def _():
                copy(out_ref.at[s], s, 2, right, q).wait_send()


def row_gather(placed, nz):
    groups = 2 * nz
    return pl.pallas_call(
        functools.partial(gather_kernel, nz, RELAY_PARTS),
        out_shape=jax.ShapeDtypeStruct((groups,) + placed.shape, placed.dtype),
        in_specs=[pl.BlockSpec(memory_space=pltpu.VMEM)],
        out_specs=pl.BlockSpec(memory_space=pltpu.VMEM),
        scratch_shapes=[
            pltpu.SemaphoreType.DMA(()),
            pltpu.SemaphoreType.DMA((groups, RELAY_PARTS, 3)),
            pltpu.SemaphoreType.DMA((groups, RELAY_PARTS)),
        ],
        compiler_params=pltpu.CompilerParams(collective_id=0, has_side_effects=True),
    )(placed)


def exchange_kernel(nb, nxy, src_ref, mine_ref, out_ref, other_ref, local_sem, send_sem, recv_sem,
                    pair_sem):
    zl = lax.axis_index("zl")
    c = lax.axis_index("core")
    me = lax.axis_index("zh") * nxy + lax.axis_index("xy")

    def peer(b):
        return (zl, c, b // nxy, lax.rem(b, nxy))

    barrier = pltpu.get_barrier_semaphore()

    def greet(p, carry):
        pl.semaphore_signal(barrier, 1, device_id=peer(lax.rem(me + p, nb)), device_id_type=MESH)
        return carry

    lax.fori_loop(1, nb, greet, 0)
    pl.semaphore_wait(barrier, nb - 1)

    mine = pltpu.make_async_copy(src_ref.at[me], out_ref.at[me], local_sem)
    mine.start()

    def copy(p, dest):
        return pltpu.make_async_remote_copy(
            src_ref=src_ref.at[dest],
            dst_ref=out_ref.at[me],
            send_sem=send_sem.at[p],
            recv_sem=recv_sem.at[me],
            device_id=peer(dest),
            device_id_type=MESH,
        )

    def send(p, carry):
        step = lax.rem(p + nb // 2 - 2, nb - 1) + 1
        copy(step, lax.rem(me + step, nb)).start()
        return carry

    lax.fori_loop(1, nb, send, 0)

    twin = lax.rem(me + nb // 2, nb)
    pair_copy = pltpu.make_async_remote_copy(
        src_ref=mine_ref,
        dst_ref=other_ref,
        send_sem=pair_sem.at[0],
        recv_sem=pair_sem.at[1],
        device_id=peer(twin),
        device_id_type=MESH,
    )
    pair_copy.start()

    def receive(p, carry):
        source = lax.rem(me + nb - p, nb)
        pltpu.make_async_remote_copy(
            src_ref=src_ref.at[source],
            dst_ref=out_ref.at[source],
            send_sem=send_sem.at[p],
            recv_sem=recv_sem.at[source],
            device_id=peer(source),
            device_id_type=MESH,
        ).wait_recv()
        return carry

    lax.fori_loop(1, nb, receive, 0)
    mine.wait()
    pair_copy.wait_recv()
    pair_copy.wait_send()

    def sent(p, carry):
        copy(p, lax.rem(me + p, nb)).wait_send()
        return carry

    lax.fori_loop(1, nb, sent, 0)


def bulk_exchange(outgoing, mine_t, nb, nxy):
    return pl.pallas_call(
        functools.partial(exchange_kernel, nb, nxy),
        out_shape=(
            jax.ShapeDtypeStruct(outgoing.shape, outgoing.dtype),
            jax.ShapeDtypeStruct(mine_t.shape, mine_t.dtype),
        ),
        in_specs=[pl.BlockSpec(memory_space=pltpu.VMEM)] * 2,
        out_specs=(pl.BlockSpec(memory_space=pltpu.VMEM), pl.BlockSpec(memory_space=pltpu.VMEM)),
        scratch_shapes=[
            pltpu.SemaphoreType.DMA(()),
            pltpu.SemaphoreType.DMA((nb,)),
            pltpu.SemaphoreType.DMA((nb,)),
            pltpu.SemaphoreType.DMA((2,)),
        ],
        compiler_params=pltpu.CompilerParams(collective_id=1, has_side_effects=True),
    )(outgoing, mine_t)


def local(residual_in, amplitudes, integral_tiles, tile_reader, tile_k, tile_column):
    nxy = lax.axis_size("xy")
    targets = lax.axis_size("zh") * nxy
    height, width = integral_tiles.shape[1], integral_tiles.shape[2]
    filled, local_index, slot_position = bucket_slots(
        tile_reader, tile_k, tile_column, targets, SLOT
    )
    picked = jnp.take(integral_tiles, local_index.reshape(-1), axis=0)
    picked = jnp.where(filled.reshape(-1)[:, None, None] > 0, picked, 0.0)
    label = jnp.zeros((targets, 1, width), jnp.float32).at[:, 0, :SLOT].set(
        slot_position.reshape(targets, SLOT).astype(jnp.float32)
    )
    outgoing = jnp.concatenate([picked.reshape(targets, SLOT * height, width), label], axis=1)
    arrived, other_t = bulk_exchange(outgoing, amplitudes.T, targets, nxy)
    position = arrived[:, SLOT * height, :SLOT].reshape(-1).astype(jnp.int32)
    arrived = arrived[:, : SLOT * height, :].reshape(targets * SLOT, height * width)
    table = (position[None, :] == jnp.arange(KT * CT, dtype=jnp.int32)[:, None]).astype(jnp.float32)
    placed = jnp.dot(table, arrived, precision=lax.Precision.HIGHEST)
    placed = placed.reshape(KT, CT, height, width).transpose(0, 2, 1, 3).reshape(KT * height, CT * width)
    nz = lax.axis_size("zl")
    gathered = row_gather(placed, nz)
    dense = gathered.reshape(-1, CT * width)
    other = other_t.T
    lower = lax.axis_index("zh") == 0
    pair = jnp.stack([jnp.where(lower, amplitudes, other), jnp.where(lower, other, amplitudes)])
    blocks = lax.all_gather(pair, "xy", axis=0, tiled=False)
    rows, own_cols = amplitudes.shape
    amps = blocks.transpose(2, 1, 0, 3).reshape(rows, targets * own_cols)
    groups = gathered.shape[0]
    amps = amps.reshape(rows, KT, groups, height).transpose(0, 2, 1, 3).reshape(rows, -1)
    return residual_in + jnp.dot(amps, dense, precision=lax.Precision.HIGH)


def solution(mesh):
    row_size = mesh.shape["row"]
    bulk_size = mesh.shape["bulk"]
    devices = np.asarray(mesh.devices).reshape(row_size // 2, 2, Z_HALVES, bulk_size // Z_HALVES)
    inner = Mesh(devices, ("zl", "core", "zh", "xy"))
    row = ("zl", "core")
    bulk = ("zh", "xy")
    placed = (
        P(row, bulk),
        P(row, bulk),
        P(bulk, row, None),
        P(bulk, None),
        P(bulk),
        P(bulk),
    )
    return jax.shard_map(
        local, mesh=inner, in_specs=placed, out_specs=P(row, bulk), check_vma=False
    )
```
